256 devices in a mesh: dp: 4 (over x), expert: 64 (over y, z, core).
Axes of the slice: x: 4, y: 4, z: 8, core: 2. Of those that a mesh axis runs over, the one named last changes fastest.
Arguments:
- tokens: bfloat16 [32768, 2048], P(('dp', 'expert')), may hold values from -6 to 6
- tangent: bfloat16 [32768, 2048], P(('dp', 'expert')), may hold values from -16 to 16
- routes: int32 [32768, 4], P(('dp', 'expert')), may hold values from 0 to 63, all different within a row; in each aligned block of 128 rows (0 to 127, 128 to 255, ...) at most 9 rows name the same one
- gates: float32 [32768, 4], P(('dp', 'expert')), may hold values from 0.05 to 0.5
- w_gate: bfloat16 [64, 2048, 768], P('expert'), may hold values from -0.125 to 0.125
- w_up: bfloat16 [64, 2048, 768], P('expert'), may hold values from -0.125 to 0.125
- w_down: bfloat16 [64, 768, 2048], P('expert'), may hold values from -0.21875 to 0.21875
Outputs:
- product: float32 [32768, 2048], P(('dp', 'expert'))
The draws below stay inside these ranges and needn't reach their ends.
Inputs may be any that keep to these rules, and one draw needn't show every extreme that they name: `routes`: among the 512 pairs of the rows of one device, no expert is named more than 9 times, a bound that some block reaches.
All inputs are finite; a program needn't handle non-finite values.
Results may differ from the reference program's by a relative error of at most 0.005.
Values may be sent and summed in bfloat16 or wider, within the bound.
A program may use at most 128 MiB of HBM per device.

```python
import math
import jax
import jax.numpy as jnp
import numpy as np
from jax import lax

D = 2048
FF = 768
TOP = 4
TOK_DEV = 128
EXPERTS = 64
CAP = 9
TOKENS = 32768
N_DP = 4
N_EXPERT = 64


def draw_tangent(key, part):
    position = jnp.arange(TOKENS, dtype=jnp.float32) / TOKENS
    rising = 1.0 + 2.0 * position
    values = jnp.clip(jax.random.normal(key, (TOKENS, D), jnp.float32), -4.0, 4.0)
    return (values * rising[:, None]).astype(jnp.bfloat16)


def block_levels(stream_key, extent, cuts, low, top_value):
    gain = 1.0
    for dim, parts in cuts:
        draws = jax.random.uniform(jax.random.fold_in(jax.random.fold_in(stream_key, 6), dim), (parts,), jnp.float32, low / len(cuts), top_value / len(cuts))
        gain = gain * jnp.repeat(jnp.exp(draws), extent[dim] // parts).reshape((-1,) + (1,) * (len(extent) - 1 - dim))
    return gain


def shared_out(rng, own, number, rows, number_of, top, limit, lean):
    sequence = jax.random.permutation(rng, number_of)
    crowded, common = shares(number_of, rows * top, limit, lean, True), shares(number_of, rows * top, limit, lean, False)
    places = jnp.arange(number_of)

    def named(sizes, offset_by):
        used = int((sizes > 0).sum())
        fixed = max(1, used // 4)
        moved = fixed + (places - fixed + offset_by * (used - fixed)) % max(1, number_of - fixed)
        return jnp.zeros((number_of,), jnp.int32).at[sequence[jnp.where(places < fixed, places, moved)]].set(jnp.asarray(sizes, jnp.int32))

    sizes = jnp.where(number % 4 == 0, named(crowded, number // 4), named(common, number - number // 4 - 1))
    mixed = jax.random.permutation(jax.random.fold_in(own, 3), number_of)
    donor, sink = mixed[0:number_of // 2 * 2:2], mixed[1:number_of // 2 * 2:2]
    slack = jnp.minimum(sizes[donor] - 1, limit - sizes[sink]) // 2
    slack = jnp.where((donor == sequence[0]) | (sink == sequence[0]) | (sizes[sink] == 0), 0, jnp.maximum(slack, 0))
    moved = jax.random.randint(jax.random.fold_in(own, 4), (number_of // 2,), 0, 1 << 20) % (slack + 1)
    sizes = sizes.at[donor].add(-moved).at[sink].add(moved)
    members = jnp.searchsorted(jnp.cumsum(sizes), jnp.arange(rows * top), side="right").astype(jnp.int32)
    table = members.reshape(top, rows).T
    table = table[jax.random.permutation(jax.random.fold_in(own, 1), rows)]
    offset_by = jax.random.randint(jax.random.fold_in(own, 2), (rows, 1), 0, top)
    return jnp.take_along_axis(table, (jnp.arange(top)[None, :] + offset_by) % top, axis=1)


def shares(amount, total, bound, lean, full):
    weights = [(1 << 20) // math.isqrt(standing ** lean) + 1 for standing in range(1, amount + 1)]
    largest = bound if full else min(bound, max(-(-total // amount), total * weights[0] // sum(weights)))
    least = 1 if total - largest >= amount - 1 else 0
    counts, surplus = [largest] + [least] * (amount - 1), total - largest - least * (amount - 1)
    while surplus > 0:
        candidates = [i for i in range(1, amount) if counts[i] < largest] or [i for i in range(1, amount) if counts[i] < bound]
        mass, left = sum([weights[i] for i in candidates]), surplus
        for i in candidates:
            addition = min(bound - counts[i], max(1, left * weights[i] // mass), surplus)
            counts[i] = counts[i] + addition
            surplus = surplus - addition
    return np.array(counts)


def scatter_about(own_key, dims, deviation, most, pieces=(), kind=jnp.bfloat16):
    gain = block_levels(own_key, dims, pieces, -0.22, 0.18) if pieces else 1.0
    array = jax.random.normal(own_key, dims, jnp.float32) * deviation * gain
    return jnp.minimum(jnp.maximum(array, -most), most).astype(kind)


def setup_inputs(seed: int = 0) -> dict:
    key_list = jax.random.split(jax.random.key(seed), 8)
    tokens = scatter_about(key_list[0], (TOKENS, D), 1.0, 6.0, ((0, 256),))
    tangent = draw_tangent(jax.random.fold_in(key_list[7], 71), 0)
    routes_keys = jax.random.split(jax.random.fold_in(key_list[2], 1), TOKENS // TOK_DEV)
    routes_turns = jax.random.permutation(jax.random.fold_in(key_list[2], 3), TOKENS // TOK_DEV)
    routes = jax.vmap(lambda own, number: shared_out(jax.random.fold_in(key_list[2], 2), own, number, TOK_DEV, EXPERTS, TOP, CAP, 2))(routes_keys, routes_turns).reshape((TOKENS, TOP))
    gates = jnp.clip(0.05 + 0.45 * jax.random.uniform(key_list[3], (TOKENS, TOP), jnp.float32) ** block_levels(key_list[3], (TOKENS, TOP), ((0, 256),), -0.2, 0.2), 0.05, 0.5)
    w_gate = scatter_about(key_list[4], (EXPERTS, D, FF), D ** -0.5, 0.125, ((0, 64),))
    w_up = scatter_about(key_list[5], (EXPERTS, D, FF), D ** -0.5, 0.125, ((0, 64),))
    w_down = scatter_about(key_list[6], (EXPERTS, FF, D), FF ** -0.5, 0.21875, ((0, 64),))
    return {"tokens": tokens, "tangent": tangent, "routes": routes, "gates": gates, "w_gate": w_gate, "w_up": w_up, "w_down": w_down}


def reference(tokens, tangent, routes, gates, w_gate, w_up, w_down):
    most_rows = CAP * N_DP * N_EXPERT
    flat_routes = routes.reshape(-1).astype(jnp.int32)
    flat_gates = gates.reshape(-1)
    pair_token = jnp.arange(TOKENS * TOP, dtype=jnp.int32) // TOP
    experts_iota = jnp.arange(EXPERTS, dtype=jnp.int32)

    def select(expert_id):
        chosen = flat_routes == expert_id
        index = jnp.nonzero(chosen, size=most_rows, fill_value=0)[0].astype(jnp.int32)
        number = jnp.sum(chosen.astype(jnp.int32))
        valid = jnp.arange(most_rows, dtype=jnp.int32) < number
        rows_tok = pair_token[index]
        gate_vals = jnp.where(valid, flat_gates[index], jnp.float32(0.0))
        return (rows_tok, gate_vals)

    def project(x_rows, gate_w, up_w):
        return (jnp.dot(x_rows, gate_w, preferred_element_type=jnp.float32), jnp.dot(x_rows, up_w, preferred_element_type=jnp.float32))

    def forward_step(carry, inputs):
        expert_id, gate_w, up_w, down_w = inputs
        rows_tok, gate_vals = select(expert_id)
        pre_a, pre_b = project(tokens[rows_tok], gate_w, up_w)
        tan_a, tan_b = project(tangent[rows_tok], gate_w, up_w)
        sigma = jax.nn.sigmoid(pre_a)
        act = pre_a * sigma
        slope = sigma * (1.0 + pre_a * (1.0 - sigma))
        hidden_tangent = (slope * tan_a * pre_b + act * tan_b).astype(jnp.bfloat16)
        pair_tangent = jnp.dot(hidden_tangent, down_w, preferred_element_type=jnp.float32).astype(jnp.bfloat16)
        carry = carry.at[rows_tok].add(gate_vals[:, None] * pair_tangent.astype(jnp.float32))
        return (carry, None)
    jv_vals, _ = lax.scan(forward_step, tangent.astype(jnp.float32), (experts_iota, w_gate, w_up, w_down))

    def backward_step(carry, inputs):
        expert_id, gate_w, up_w, down_w = inputs
        rows_tok, gate_vals = select(expert_id)
        pre_a, pre_b = project(tokens[rows_tok], gate_w, up_w)
        sigma = jax.nn.sigmoid(pre_a)
        act = pre_a * sigma
        slope = sigma * (1.0 + pre_a * (1.0 - sigma))
        pair_cotangent = (gate_vals[:, None] * jv_vals[rows_tok]).astype(jnp.bfloat16)
        back_vals = jnp.dot(pair_cotangent, down_w.T, preferred_element_type=jnp.float32)
        grad_gate = (back_vals * pre_b * slope).astype(jnp.bfloat16)
        grad_up = (back_vals * act).astype(jnp.bfloat16)
        pair_grad = (jnp.dot(grad_gate, gate_w.T, preferred_element_type=jnp.float32) + jnp.dot(grad_up, up_w.T, preferred_element_type=jnp.float32)).astype(jnp.bfloat16)
        carry = carry.at[rows_tok].add(pair_grad.astype(jnp.float32))
        return (carry, None)
    summed, _ = lax.scan(backward_step, jv_vals, (experts_iota, w_gate, w_up, w_down))
    curvature = jnp.sum(jv_vals * jv_vals)
    return summed * lax.rsqrt(curvature / (TOKENS * D) + 1e-06)
```

```python
import functools
import jax
import jax.numpy as jnp
from jax import lax
from jax.experimental import pallas as pl
from jax.experimental.pallas import tpu as pltpu
from jax.sharding import PartitionSpec as P

MESH = pl.DeviceIdType.MESH
F32 = jnp.float32
BF16 = jnp.bfloat16
CAP = 9
STG = 3


def body(
    ny, nz, nx, dims, x_hbm, v_hbm, rt_ref, gt_ref, wg_hbm, wu_hbm, wd_hbm, out_hbm,
    wg, wu, wd, g, r, sel, selt, acc, hid, gru, ret, yb, rs, stg, rstg, jvf, ostg,
    metas, metar, gsend, grecv, red, ssacc,
    load_sem, w_sem, ag_r, ag_s, y_r, y_s, rt_r, rt_s, rs_r, rs_s, o_sem, meta_sem, gate_sem, red_sem,
):
    tok, width, rows, nch, ff = dims
    peers = 2 * ny
    half = nz // 2
    total = peers * rows
    me = lax.axis_index("expert")
    mx = lax.axis_index("dp")
    my = me // (2 * nz)
    mz = lax.rem(me // 2, nz)
    mc = lax.rem(me, 2)
    mp = my * 2 + mc

    def zdev(zt):
        return my * (2 * nz) + zt * 2 + mc

    def pdev(d):
        return (d // 2) * (2 * nz) + mz * 2 + lax.rem(d, 2)

    def zoff(k):
        return lax.rem(mz + (k + nz), nz)

    right = zdev(zoff(1))
    left = zdev(zoff(-1))

    def local(src, dst, sem):
        return pltpu.make_async_copy(src, dst, sem)

    def remote(src, dst, ssem, rsem, dev):
        return pltpu.make_async_remote_copy(
            src_ref=src, dst_ref=dst, send_sem=ssem, recv_sem=rsem,
            device_id={"expert": dev}, device_id_type=MESH,
        )

    def load(i, hbm, ch):
        return local(hbm.at[:, pl.ds(ch * width, width)], g.at[i, mz], load_sem.at[i])

    for ch in range(nch):
        load(2 * ch, x_hbm, ch).start()
        load(2 * ch + 1, v_hbm, ch).start()
    for ch in range(nch):
        local(wg_hbm.at[0, pl.ds(ch * width, width), :], wg.at[ch], w_sem.at[0]).start()
        local(wu_hbm.at[0, pl.ds(ch * width, width), :], wu.at[ch], w_sem.at[1]).start()
    for ch in range(nch):
        local(wd_hbm.at[0, :, pl.ds(ch * width, width)], wd.at[ch], w_sem.at[2]).start()

    barrier = pltpu.get_barrier_semaphore()
    for k in range(1, nz):
        pl.semaphore_signal(barrier, inc=1, device_id={"expert": zdev(zoff(k))}, device_id_type=MESH)
    for k in range(1, peers):
        pl.semaphore_signal(
            barrier, inc=1, device_id={"expert": pdev(lax.rem(mp + k, peers))}, device_id_type=MESH
        )
    for k in range(1, nx):
        pl.semaphore_signal(
            barrier, inc=1, device_id={"dp": lax.rem(mx + k, nx)}, device_id_type=MESH
        )

    pshift = peers.bit_length() - 1
    row = lax.broadcasted_iota(jnp.int32, (nz * peers, tok), 0)
    zrow = lax.shift_right_logical(row, pshift)
    drow = jnp.bitwise_and(row, peers - 1)
    expert = lax.shift_right_logical(drow, 1) * (2 * nz) + zrow * 2 + jnp.bitwise_and(drow, 1)
    named = jnp.zeros((nz * peers, tok), F32)
    weight = jnp.zeros((nz * peers, tok), F32)
    for k in range(rt_ref.shape[0]):
        hit = jnp.broadcast_to(rt_ref[k : k + 1, :], expert.shape) == expert
        named = named + jnp.where(hit, 1.0, 0.0)
        weight = weight + jnp.where(hit, jnp.broadcast_to(gt_ref[k : k + 1, :], expert.shape), 0.0)
    earlier = lax.broadcasted_iota(jnp.int32, (tok, tok), 0) < lax.broadcasted_iota(
        jnp.int32, (tok, tok), 1
    )
    rank = jnp.dot(
        named.astype(BF16), jnp.where(earlier, 1.0, 0.0).astype(BF16), preferred_element_type=F32
    )
    base = (mz * CAP).astype(F32)
    code = jnp.where(named > 0.5, rank + base, -1.0)
    for zt in range(nz):
        metas[zt, 0:peers, :] = code[zt * peers : (zt + 1) * peers]
        metas[zt, peers : 2 * peers, :] = weight[zt * peers : (zt + 1) * peers]
    metar[mz] = metas[mz]

    @pl.loop(0, total // 16)
    def _(q):
        for m in range(4):
            acc[m, pl.ds(pl.multiple_of(q * 16, 16), 16), :] = jnp.zeros((16, ff), F32)

    ssacc[...] = jnp.zeros(ssacc.shape, F32)
    pl.semaphore_wait(barrier, (nz - 1) + (peers - 1) + (nx - 1))

    for k in range(1, nz):
        zt = zoff(k)
        remote(metas.at[zt], metar.at[mz], meta_sem.at[0], meta_sem.at[1], zdev(zt)).start()

    def ag_send(i, slot, zs, dev):
        remote(g.at[i, zs], g.at[i, zs], ag_s.at[i], ag_r.at[i, slot], dev).start()

    def ag_wait(i, slot):
        remote(g.at[i, mz], g.at[i, mz], ag_s.at[i], ag_r.at[i, slot], right).wait_recv()

    def ag_first(i):
        ag_send(i, 0, mz, right)
        ag_send(i, 1, mz, left)

    def ag_mid(i, s):
        ag_wait(i, 2 * (s - 2))
        ag_send(i, 2 * (s - 1), zoff(-(s - 1)), right)
        ag_wait(i, 2 * (s - 2) + 1)
        ag_send(i, 2 * (s - 1) + 1, zoff(s - 1), left)

    def ag_far(i, par):
        ag_wait(i, 2 * (half - 2))
        ag_wait(i, 2 * (half - 2) + 1)
        zs = jnp.where(par == 0, zoff(-(half - 1)), zoff(half - 1))
        ag_send(i, 2 * half - 2, zs, jnp.where(par == 0, right, left))

    def ag_done(i):
        ag_wait(i, 2 * half - 2)

    def ag_drain(i):
        local(g.at[i, pl.ds(0, nz - 1)], g.at[i, pl.ds(0, nz - 1)], ag_s.at[i]).wait()

    def dispatch(i, slot):
        tokens = g[i].reshape(nz * tok, width)
        for d in range(peers):
            stg[slot, d] = jnp.dot(
                sel[d * rows : (d + 1) * rows, :], tokens, preferred_element_type=F32
            ).astype(BF16)

    def dispatch_send(i, slot):
        for k in range(1, peers):
            d = lax.rem(mp + k, peers)
            remote(stg.at[slot, d], r.at[i, mp], y_s.at[slot], y_r.at[i], pdev(d)).start()
        local(stg.at[slot, mp], r.at[i, mp], y_r.at[i]).start()

    def dispatch_wait(i, slot):
        local(r.at[i], r.at[i], y_r.at[i]).wait()
        local(
            stg.at[slot, pl.ds(0, peers - 1)], stg.at[slot, pl.ds(0, peers - 1)], y_s.at[slot]
        ).wait()

    def return_send(j, slot):
        for k in range(1, peers):
            d = lax.rem(mp + k, peers)
            remote(rstg.at[slot, d], ret.at[j, mp], rt_s.at[slot], rt_r.at[j], pdev(d)).start()
        local(rstg.at[slot, mp], ret.at[j, mp], rt_r.at[j]).start()

    def combine(j, slot):
        local(ret.at[j], ret.at[j], rt_r.at[j]).wait()
        local(
            rstg.at[slot, pl.ds(0, peers - 1)], rstg.at[slot, pl.ds(0, peers - 1)], rt_s.at[slot]
        ).wait()
        back_rows = ret[j].reshape(total, width)
        for zs in range(nz):
            yb[j, zs] = jnp.dot(
                selt[zs * tok : (zs + 1) * tok, :], back_rows, preferred_element_type=F32
            ).astype(BF16)

    far = 2 * (half - 1)

    def rs_send(j, src, slot, dev):
        remote(src, rs.at[j, slot], rs_s.at[j], rs_r.at[j, slot], dev).start()

    def rs_wait(j, slot):
        remote(rs.at[j, slot], rs.at[j, slot], rs_s.at[j], rs_r.at[j, slot], right).wait_recv()

    def rs_add(j, slot, zd):
        rs[j, slot] = (rs[j, slot].astype(F32) + yb[j, zd].astype(F32)).astype(BF16)

    def rs_first(j, par):
        rs_send(j, yb.at[j, zoff(half)], far, jnp.where(par == 0, right, left))
        zd = jnp.where(par == 0, zoff(-(half - 1)), zoff(half - 1))
        rs_send(j, yb.at[j, zd], 1 - par, jnp.where(par == 0, left, right))

    def rs_second(j, par):
        rs_wait(j, far)
        rs_add(j, far, jnp.where(par == 0, zoff(half - 1), zoff(-(half - 1))))
        rs_send(j, rs.at[j, far], par, jnp.where(par == 0, right, left))

    def rs_mid(j, s):
        rs_wait(j, 2 * (s - 2))
        rs_add(j, 2 * (s - 2), zoff(half - s))
        rs_wait(j, 2 * (s - 2) + 1)
        rs_add(j, 2 * (s - 2) + 1, zoff(-(half - s)))
        rs_send(j, rs.at[j, 2 * (s - 2)], 2 * (s - 1), right)
        rs_send(j, rs.at[j, 2 * (s - 2) + 1], 2 * (s - 1) + 1, left)

    def rs_final(j):
        rs_wait(j, far - 2)
        rs_wait(j, far - 1)
        return (
            rs[j, far - 2].astype(F32) + rs[j, far - 1].astype(F32) + yb[j, mz].astype(F32)
        )

    def rs_drain(j):
        local(rs.at[j], rs.at[j], rs_s.at[j]).wait()

    def at(lag, count, tick, fn):
        i = tick - lag

        @pl.when((i >= 0) & (i < count))
        def _():
            fn(i)

    nitem = 2 * nch

    def first(i):
        load(i, x_hbm, 0).wait()
        ag_first(i)

    def products(i):
        dispatch_wait(i, lax.rem(i, STG))
        ch = i // 2
        m = lax.rem(i, 2) * 2
        got = r[i].reshape(total, width)
        for n in range(ff // width):
            cols = slice(n * width, (n + 1) * width)
            acc[m, :, cols] += jnp.dot(got, wg[ch, :, cols], preferred_element_type=F32)
            acc[m + 1, :, cols] += jnp.dot(got, wu[ch, :, cols], preferred_element_type=F32)

    def spread(i):
        ag_done(i)
        dispatch(i, lax.rem(i, STG))
        dispatch_send(i, lax.rem(i, STG))

    def build():
        local(metar.at[pl.ds(0, nz - 1)], metar.at[pl.ds(0, nz - 1)], meta_sem.at[1]).wait()
        local(metas.at[pl.ds(0, nz - 1)], metas.at[pl.ds(0, nz - 1)], meta_sem.at[0]).wait()
        slot_id = lax.broadcasted_iota(jnp.int32, (peers, rows, tok), 1).astype(F32)
        slot_id = slot_id.reshape(total, tok)
        gates = jnp.zeros((total, tok), F32)
        for zs in range(nz):
            q = jnp.broadcast_to(metar[zs, 0:peers, :][:, None, :], (peers, rows, tok))
            w = jnp.broadcast_to(metar[zs, peers : 2 * peers, :][:, None, :], (peers, rows, tok))
            same = q.reshape(total, tok) == slot_id
            one = jnp.where(same, 1.0, 0.0)
            sel[:, zs * tok : (zs + 1) * tok] = one.astype(BF16)
            selt[zs * tok : (zs + 1) * tok, :] = one.T.astype(BF16)
            gates = gates + jnp.where(same, w.reshape(total, tok), 0.0)
        gate = jnp.broadcast_to(jnp.sum(gates, axis=1, keepdims=True), (total, tok))
        gsend[...] = gate.reshape(peers, rows, tok)
        for k in range(1, peers):
            d = lax.rem(mp + k, peers)
            remote(gsend.at[d], grecv.at[mp], gate_sem.at[0], gate_sem.at[1], pdev(d)).start()
        local(gsend.at[mp], grecv.at[mp], gate_sem.at[1]).start()

    def tick_a(t, carry):
        at(half - 1, nitem, t, lambda i: ag_far(i, lax.rem(i, 2)))
        for s in range(half - 1, 1, -1):
            at(s - 1, nitem, t, lambda i, s=s: ag_mid(i, s))
        at(0, nitem, t, first)

        @pl.when(t == half - 1)
        def _():
            build()

        at(half, nitem, t, spread)

        @pl.when(t == half + 1)
        def _():
            for q, (hbm, vm) in enumerate(((wg_hbm, wg), (wu_hbm, wu), (wd_hbm, wd))):
                local(vm, vm, w_sem.at[q]).wait()

        at(half + 2, nitem, t, products)
        at(half + 2, nitem, t, ag_drain)
        return carry

    lax.fori_loop(0, nitem + half + 2, tick_a, 0)

    local(grecv, grecv, gate_sem.at[1]).wait()
    local(gsend.at[pl.ds(0, peers - 1)], gsend.at[pl.ds(0, peers - 1)], gate_sem.at[0]).wait()

    @pl.loop(0, total // 16)
    def _(q):
        at_rows = pl.ds(pl.multiple_of(q * 16, 16), 16)
        a = acc[0, at_rows, :]
        b = acc[1, at_rows, :]
        s = jax.nn.sigmoid(a)
        act = a * s
        slope_b = s * (1.0 + a * (1.0 - s)) * b
        hid[at_rows, :] = (slope_b * acc[2, at_rows, :] + act * acc[3, at_rows, :]).astype(BF16)
        acc[0, at_rows, :] = act
        acc[1, at_rows, :] = slope_b
        acc[2, at_rows, :] = jnp.zeros((16, ff), F32)

    def gate_lanes():
        gl = grecv[...].reshape(total, tok)
        return jnp.concatenate([gl] * (width // tok), axis=1)

    def tangent_out(j):
        slot = lax.rem(j, STG)
        pt = jnp.dot(hid[...], wd[j], preferred_element_type=F32) * gate_lanes()
        rstg[slot] = pt.astype(BF16).reshape(peers, rows, width)
        return_send(j, slot)

    def home(j):
        combine(j, lax.rem(j, STG))
        rs_first(j, lax.rem(j, 2))

    def finish_jv(j):
        jv = rs_final(j) + g[2 * j + 1, mz].astype(F32)
        jvf[j] = jv
        ssacc[...] += jv * jv
        g[2 * j, mz] = jv.astype(BF16)
        ag_first(2 * j)

    def spread_jv(j):
        rs_drain(j)
        ag_done(2 * j)
        dispatch(2 * j, lax.rem(j, STG))
        dispatch_send(2 * j, lax.rem(j, STG))

    contract_last = (((1,), (1,)), ((), ()))

    def back(j):
        dispatch_wait(2 * j, lax.rem(j, STG))
        ag_drain(2 * j)
        got = r[2 * j].reshape(total, width)
        for n in range(ff // width):
            cols = slice(n * width, (n + 1) * width)
            acc[2, :, cols] += lax.dot_general(
                got, wd[j, cols, :], contract_last, preferred_element_type=F32
            )

    rl = 2
    al = rl + half

    def tick_b(t, carry):
        at(al + half - 1, nch, t, lambda j: ag_far(2 * j, lax.rem(j, 2)))
        for s in range(half - 1, 1, -1):
            at(al + s - 1, nch, t, lambda j, s=s: ag_mid(2 * j, s))
        for s in range(half - 1, 1, -1):
            at(rl + s, nch, t, lambda j, s=s: rs_mid(j, s))
        at(rl + 1, nch, t, lambda j: rs_second(j, lax.rem(j, 2)))
        at(al, nch, t, finish_jv)
        at(0, nch, t, tangent_out)
        at(al + half, nch, t, spread_jv)
        at(rl, nch, t, home)
        at(al + half + 2, nch, t, back)
        return carry

    lax.fori_loop(0, nch + al + half + 2, tick_b, 0)

    def exchange(stage, me_slot, count, dev_of):
        for k in range(1, count):
            d = lax.rem(me_slot + k, count)
            pltpu.make_async_remote_copy(
                src_ref=red.at[stage, me_slot], dst_ref=red.at[stage, me_slot],
                send_sem=red_sem.at[0, stage], recv_sem=red_sem.at[1, stage],
                device_id=dev_of(d), device_id_type=MESH,
            ).start()

    def gathered(stage, count):
        span = red.at[stage, pl.ds(0, count - 1)]
        local(span, span, red_sem.at[1, stage]).wait()
        local(span, span, red_sem.at[0, stage]).wait()
        value = red[stage, 0]
        for k in range(1, count):
            value = value + red[stage, k]
        return value

    part = jnp.sum(jnp.sum(ssacc[...], axis=1, keepdims=True), axis=0, keepdims=True)
    red[0, mp] = jnp.broadcast_to(part, (8, 128))
    if peers > 1:
        exchange(0, mp, peers, lambda d: {"expert": pdev(d)})

    @pl.loop(0, total // 16)
    def _(q):
        at_rows = pl.ds(pl.multiple_of(q * 16, 16), 16)
        gl = grecv[q // (rows // 16), pl.ds(pl.multiple_of(lax.rem(q, rows // 16) * 16, 16), 16), :]
        bk = acc[2, at_rows, :] * jnp.concatenate([gl] * (ff // tok), axis=1)
        gru[0, at_rows, :] = (bk * acc[1, at_rows, :]).astype(BF16)
        gru[1, at_rows, :] = (bk * acc[0, at_rows, :]).astype(BF16)

    red[1, mz] = gathered(0, peers)
    exchange(1, mz, nz, lambda d: {"expert": zdev(d)})

    def grad_out(j):
        slot = lax.rem(j, STG)
        pg = lax.dot_general(gru[0], wg[j], contract_last, preferred_element_type=F32)
        pg = pg + lax.dot_general(gru[1], wu[j], contract_last, preferred_element_type=F32)
        rstg[slot] = pg.astype(BF16).reshape(peers, rows, width)
        return_send(j, slot)

    def out_copy(j, slot):
        return local(ostg.at[slot], out_hbm.at[:, pl.ds(pl.multiple_of(j * width, width), width)], o_sem.at[slot])

    def finish_out(j):
        slot = lax.rem(j, 2)

        @pl.when(j >= 2)
        def _():
            out_copy(j - 2, slot).wait()

        mean = red[3, 0][0:1, 0:1] * (1.0 / (tok * nx * ny * nz * 2.0 * nch * width))
        scale = jnp.broadcast_to(lax.rsqrt(mean + 1e-06), (tok, width))
        ostg[slot] = (rs_final(j) + jvf[j]) * scale
        out_copy(j, slot).start()

    def tick_d(t, carry):
        for s in range(half - 1, 1, -1):
            at(rl + s, nch, t, lambda j, s=s: rs_mid(j, s))
        at(rl + 1, nch, t, lambda j: rs_second(j, lax.rem(j, 2)))
        at(0, nch, t, grad_out)
        at(rl, nch, t, home)

        @pl.when(t == rl + 1)
        def _():
            red[2, mx] = gathered(1, nz)
            if nx > 1:
                exchange(2, mx, nx, lambda d: {"dp": d})

        @pl.when(t == al)
        def _():
            red[3, 0] = gathered(2, nx) if nx > 1 else red[2, 0]

        at(al, nch, t, finish_out)
        return carry

    lax.fori_loop(0, nch + al, tick_d, 0)
    for j in range(nch):
        rs_drain(j)
    for j in range(max(0, nch - 2), nch):
        out_copy(j, j % 2).wait()


def shards(ny, nz, nx, tokens, tangent, routes, gates, w_gate, w_up, w_down):
    tok, depth = tokens.shape
    ff = w_gate.shape[2]
    width = 256
    nch = depth // width
    peers = 2 * ny
    rows = -(-(nz * CAP) // 16) * 16
    total = peers * rows
    slots = max(nz, peers, nx)
    dma = pltpu.SemaphoreType.DMA
    scratch = [
        pltpu.VMEM((nch, width, ff), BF16),
        pltpu.VMEM((nch, width, ff), BF16),
        pltpu.VMEM((nch, ff, width), BF16),
        pltpu.VMEM((2 * nch, nz, tok, width), BF16),
        pltpu.VMEM((2 * nch, peers, rows, width), BF16),
        pltpu.VMEM((total, nz * tok), BF16),
        pltpu.VMEM((nz * tok, total), BF16),
        pltpu.VMEM((4, total, ff), F32),
        pltpu.VMEM((total, ff), BF16),
        pltpu.VMEM((2, total, ff), BF16),
        pltpu.VMEM((nch, peers, rows, width), BF16),
        pltpu.VMEM((nch, nz, tok, width), BF16),
        pltpu.VMEM((nch, nz - 1, tok, width), BF16),
        pltpu.VMEM((STG, peers, rows, width), BF16),
        pltpu.VMEM((STG, peers, rows, width), BF16),
        pltpu.VMEM((nch, tok, width), F32),
        pltpu.VMEM((2, tok, width), F32),
        pltpu.VMEM((nz, 2 * peers, tok), F32),
        pltpu.VMEM((nz, 2 * peers, tok), F32),
        pltpu.VMEM((peers, rows, tok), F32),
        pltpu.VMEM((peers, rows, tok), F32),
        pltpu.VMEM((4, slots, 8, 128), F32),
        pltpu.VMEM((tok, width), F32),
        dma((2 * nch,)),
        dma((3,)),
        dma((2 * nch, nz - 1)),
        dma((2 * nch,)),
        dma((2 * nch,)),
        dma((STG,)),
        dma((nch,)),
        dma((STG,)),
        dma((nch, nz - 1)),
        dma((nch,)),
        dma((2,)),
        dma((2,)),
        dma((2,)),
        dma((2, 3)),
    ]
    anywhere = pl.BlockSpec(memory_space=pl.ANY)
    vmem = pl.BlockSpec(memory_space=pltpu.VMEM)
    return pl.pallas_call(
        functools.partial(body, ny, nz, nx, (tok, width, rows, nch, ff)),
        out_shape=jax.ShapeDtypeStruct((tok, depth), F32),
        in_specs=[anywhere, anywhere, vmem, vmem, anywhere, anywhere, anywhere],
        out_specs=anywhere,
        scratch_shapes=scratch,
        compiler_params=pltpu.CompilerParams(
            collective_id=0, has_side_effects=True, vmem_limit_bytes=67043328
        ),
        name="gauss_newton_moe",
    )(tokens, tangent, routes.T, gates.T, w_gate, w_up, w_down)


def build(mesh, ny, nz):
    placed = (
        P(("dp", "expert"), None),
        P(("dp", "expert"), None),
        P(("dp", "expert"), None),
        P(("dp", "expert"), None),
        P("expert", None, None),
        P("expert", None, None),
        P("expert", None, None),
    )
    return jax.shard_map(
        functools.partial(shards, ny, nz, mesh.shape["dp"]),
        mesh=mesh,
        in_specs=placed,
        out_specs=P(("dp", "expert"), None),
        check_vma=False,
    )


def solution(mesh):
    return build(mesh, 4, 8)
```

```python
import functools
import jax
import jax.numpy as jnp
from jax import lax
from jax.experimental import pallas as pl
from jax.experimental.pallas import tpu as pltpu
from jax.sharding import PartitionSpec as P

MESH = pl.DeviceIdType.MESH
F32 = jnp.float32
BF16 = jnp.bfloat16
CAP = 9
STG = 3
HA = 1
HB = 1
HD = 1
YL = 2
NS = 2


def body(
    ny, nz, nx, dims, x_hbm, v_hbm, rt_ref, gt_ref, wg_hbm, wu_hbm, wd_hbm, out_hbm,
    wg, wu, wd, g, r, sel, selt, acc, hid, gru, ret, yb, rs, stg, rstg, jvf, ostg,
    metas, metar, gsend, grecv, red, ssacc,
    load_sem, w_sem, ag_r, ag_s, y_r, y_s, rt_r, rt_s, rs_r, rs_s, o_sem, meta_sem, gate_sem, red_sem,
):
    tok, width, rows, nch, ff = dims
    peers = 2 * ny
    half = nz // 2
    nitem = 2 * nch
    total = peers * rows
    me = lax.axis_index("expert")
    mx = lax.axis_index("dp")
    my = me // (2 * nz)
    mz = lax.rem(me // 2, nz)
    mc = lax.rem(me, 2)
    mp = my * 2 + mc

    def zdev(zt):
        return my * (2 * nz) + zt * 2 + mc

    def pdev(d):
        return (d // 2) * (2 * nz) + mz * 2 + lax.rem(d, 2)

    def zoff(k):
        return lax.rem(mz + (k + nz), nz)

    right = zdev(zoff(1))
    left = zdev(zoff(-1))

    def local(src, dst, sem):
        return pltpu.make_async_copy(src, dst, sem)

    def remote(src, dst, ssem, rsem, dev):
        return pltpu.make_async_remote_copy(
            src_ref=src, dst_ref=dst, send_sem=ssem, recv_sem=rsem,
            device_id={"expert": dev}, device_id_type=MESH,
        )

    def load(i, hbm, ch):
        return local(hbm.at[:, pl.ds(ch * width, width)], g.at[i, mz], load_sem.at[i])

    for ch in range(min(2, nch)):
        load(ch, x_hbm, ch).start()

    barrier = pltpu.get_barrier_semaphore()
    for k in range(1, nz):
        pl.semaphore_signal(barrier, inc=1, device_id={"expert": zdev(zoff(k))}, device_id_type=MESH)
    for k in range(1, peers):
        pl.semaphore_signal(
            barrier, inc=1, device_id={"expert": pdev(lax.rem(mp + k, peers))}, device_id_type=MESH
        )
    for k in range(1, nx):
        pl.semaphore_signal(
            barrier, inc=1, device_id={"dp": lax.rem(mx + k, nx)}, device_id_type=MESH
        )

    pl.semaphore_wait(barrier, (nz - 1) + (peers - 1) + (nx - 1))

    part_rows = tok // NS

    def part(h):
        return pl.ds(h * part_rows, part_rows)

    def ag_send(i, slot, h, zs, dev):
        piece = g.at[i, zs, part(h)]
        remote(piece, piece, ag_s.at[i], ag_r.at[i, slot, h], dev).start()

    def ag_wait(i, slot, h):
        piece = g.at[i, mz, part(h)]
        remote(piece, piece, ag_s.at[i], ag_r.at[i, slot, h], right).wait_recv()

    def ag_first(i, h):
        ag_send(i, 0, h, mz, right)
        ag_send(i, 1, h, mz, left)

    def ag_mid(i, s, h):
        ag_wait(i, 2 * (s - 2), h)
        ag_send(i, 2 * (s - 1), h, zoff(-(s - 1)), right)
        ag_wait(i, 2 * (s - 2) + 1, h)
        ag_send(i, 2 * (s - 1) + 1, h, zoff(s - 1), left)

    def ag_far(i, h):
        par = lax.rem(i, 2)
        ag_wait(i, 2 * (half - 2), h)
        ag_wait(i, 2 * (half - 2) + 1, h)
        zs = jnp.where(par == 0, zoff(-(half - 1)), zoff(half - 1))
        ag_send(i, 2 * half - 2, h, zs, jnp.where(par == 0, right, left))

    def ag_done(i):
        for h in range(NS):
            ag_wait(i, 2 * half - 2, h)

    def ag_drain(i):
        local(g.at[i, pl.ds(0, nz - 1)], g.at[i, pl.ds(0, nz - 1)], ag_s.at[i]).wait()

    def first(i, h):
        if h == 0:
            load(i, x_hbm, 0).wait()
        ag_first(i, h)

    for h in range(NS):
        first(0, h)

    for ch in range(2, nch):
        load(ch, x_hbm, ch).start()
    for ch in range(nch):
        load(nch + ch, v_hbm, ch).start()
    for ch in range(nch):
        local(wg_hbm.at[0, pl.ds(ch * width, width), :], wg.at[ch], w_sem.at[0]).start()
        local(wu_hbm.at[0, pl.ds(ch * width, width), :], wu.at[ch], w_sem.at[1]).start()
    for ch in range(nch):
        local(wd_hbm.at[0, :, pl.ds(ch * width, width)], wd.at[ch], w_sem.at[2]).start()

    pshift = peers.bit_length() - 1
    row = lax.broadcasted_iota(jnp.int32, (nz * peers, tok), 0)
    zrow = lax.shift_right_logical(row, pshift)
    drow = jnp.bitwise_and(row, peers - 1)
    expert = lax.shift_right_logical(drow, 1) * (2 * nz) + zrow * 2 + jnp.bitwise_and(drow, 1)
    named = jnp.zeros((nz * peers, tok), F32)
    weight = jnp.zeros((nz * peers, tok), F32)
    for k in range(rt_ref.shape[0]):
        hit = jnp.broadcast_to(rt_ref[k : k + 1, :], expert.shape) == expert
        named = named + jnp.where(hit, 1.0, 0.0)
        weight = weight + jnp.where(hit, jnp.broadcast_to(gt_ref[k : k + 1, :], expert.shape), 0.0)
    earlier = lax.broadcasted_iota(jnp.int32, (tok, tok), 0) < lax.broadcasted_iota(
        jnp.int32, (tok, tok), 1
    )
    rank = jnp.dot(
        named.astype(BF16), jnp.where(earlier, 1.0, 0.0).astype(BF16), preferred_element_type=F32
    )
    base = (mz * CAP).astype(F32)
    code = jnp.where(named > 0.5, rank + base, -1.0)
    for zt in range(nz):
        metas[zt, 0:peers, :] = code[zt * peers : (zt + 1) * peers]
        metas[zt, peers : 2 * peers, :] = weight[zt * peers : (zt + 1) * peers]
    metar[mz] = metas[mz]

    @pl.loop(0, total // 16)
    def _(q):
        for m in range(4):
            acc[m, pl.ds(pl.multiple_of(q * 16, 16), 16), :] = jnp.zeros((16, ff), F32)

    ssacc[...] = jnp.zeros(ssacc.shape, F32)
    for k in range(1, nz):
        zt = zoff(k)
        remote(metas.at[zt], metar.at[mz], meta_sem.at[0], meta_sem.at[1], zdev(zt)).start()

    def dispatch(i, slot):
        tokens = g[i].reshape(nz * tok, width)
        for d in range(peers):
            stg[slot, d] = jnp.dot(
                sel[d * rows : (d + 1) * rows, :], tokens, preferred_element_type=F32
            ).astype(BF16)

    def dispatch_send(i, slot):
        for k in range(1, peers):
            d = lax.rem(mp + k, peers)
            remote(stg.at[slot, d], r.at[i, mp], y_s.at[slot], y_r.at[i], pdev(d)).start()
        local(stg.at[slot, mp], r.at[i, mp], y_r.at[i]).start()

    def dispatch_wait(i, slot):
        local(r.at[i], r.at[i], y_r.at[i]).wait()
        local(
            stg.at[slot, pl.ds(0, peers - 1)], stg.at[slot, pl.ds(0, peers - 1)], y_s.at[slot]
        ).wait()

    def return_send(j, slot):
        for k in range(1, peers):
            d = lax.rem(mp + k, peers)
            remote(rstg.at[slot, d], ret.at[j, mp], rt_s.at[slot], rt_r.at[j], pdev(d)).start()
        local(rstg.at[slot, mp], ret.at[j, mp], rt_r.at[j]).start()

    def combine(j, slot):
        local(ret.at[j], ret.at[j], rt_r.at[j]).wait()
        local(
            rstg.at[slot, pl.ds(0, peers - 1)], rstg.at[slot, pl.ds(0, peers - 1)], rt_s.at[slot]
        ).wait()
        back_rows = ret[j].reshape(total, width)
        for zs in range(nz):
            yb[j, zs] = jnp.dot(
                selt[zs * tok : (zs + 1) * tok, :], back_rows, preferred_element_type=F32
            ).astype(BF16)

    far = 2 * (half - 1)

    def rs_send(j, src, slot, h, dev):
        remote(src, rs.at[j, slot, part(h)], rs_s.at[j], rs_r.at[j, slot, h], dev).start()

    def rs_wait(j, slot, h):
        piece = rs.at[j, slot, part(h)]
        remote(piece, piece, rs_s.at[j], rs_r.at[j, slot, h], right).wait_recv()

    def rs_add(j, slot, h, zd):
        rs[j, slot, part(h)] = (
            rs[j, slot, part(h)].astype(F32) + yb[j, zd, part(h)].astype(F32)
        ).astype(BF16)

    def rs_first(j):
        par = lax.rem(j, 2)
        zd = jnp.where(par == 0, zoff(-(half - 1)), zoff(half - 1))
        for h in range(NS):
            rs_send(j, yb.at[j, zoff(half), part(h)], far, h, jnp.where(par == 0, right, left))
            rs_send(j, yb.at[j, zd, part(h)], 1 - par, h, jnp.where(par == 0, left, right))

    def rs_second(j, h):
        par = lax.rem(j, 2)
        rs_wait(j, far, h)
        rs_add(j, far, h, jnp.where(par == 0, zoff(half - 1), zoff(-(half - 1))))
        rs_send(j, rs.at[j, far, part(h)], par, h, jnp.where(par == 0, right, left))

    def rs_mid(j, s, h):
        up = 2 * (s - 2)
        rs_wait(j, up, h)
        rs_add(j, up, h, zoff(half - s))
        rs_send(j, rs.at[j, up, part(h)], up + 2, h, right)
        rs_wait(j, up + 1, h)
        rs_add(j, up + 1, h, zoff(-(half - s)))
        rs_send(j, rs.at[j, up + 1, part(h)], up + 3, h, left)

    def rs_final(j, h):
        rs_wait(j, far - 2, h)
        rs_wait(j, far - 1, h)
        return (
            rs[j, far - 2, part(h)].astype(F32)
            + rs[j, far - 1, part(h)].astype(F32)
            + yb[j, mz, part(h)].astype(F32)
        )

    def rs_drain(j):
        local(rs.at[j], rs.at[j], rs_s.at[j]).wait()

    def at(lag, count, tick, fn):
        i = tick - lag

        @pl.when((i >= 0) & (i < count))
        def _():
            fn(i)

    def products(i):
        dispatch_wait(i, lax.rem(i, STG))
        ch = lax.rem(i, nch)
        m = (i // nch) * 2
        got = r[i].reshape(total, width)
        for n in range(ff // width):
            cols = slice(n * width, (n + 1) * width)
            acc[m, :, cols] += jnp.dot(got, wg[ch, :, cols], preferred_element_type=F32)
            acc[m + 1, :, cols] += jnp.dot(got, wu[ch, :, cols], preferred_element_type=F32)

    def activate(q):
        for k in range(rows // 16):
            at_rows = pl.ds(pl.multiple_of(q * rows + k * 16, 16), 16)
            a = acc[0, at_rows, :]
            s = jax.nn.sigmoid(a)
            acc[0, at_rows, :] = a * s
            acc[1, at_rows, :] = s * (1.0 + a * (1.0 - s)) * acc[1, at_rows, :]

    def spread(i):
        ag_done(i)
        dispatch(i, lax.rem(i, STG))
        dispatch_send(i, lax.rem(i, STG))

    def build():
        local(metar.at[pl.ds(0, nz - 1)], metar.at[pl.ds(0, nz - 1)], meta_sem.at[1]).wait()
        local(metas.at[pl.ds(0, nz - 1)], metas.at[pl.ds(0, nz - 1)], meta_sem.at[0]).wait()
        slot_id = lax.broadcasted_iota(jnp.int32, (peers, rows, tok), 1).astype(F32)
        slot_id = slot_id.reshape(total, tok)
        gates = jnp.zeros((total, tok), F32)
        for zs in range(nz):
            q = jnp.broadcast_to(metar[zs, 0:peers, :][:, None, :], (peers, rows, tok))
            w = jnp.broadcast_to(metar[zs, peers : 2 * peers, :][:, None, :], (peers, rows, tok))
            same = q.reshape(total, tok) == slot_id
            one = jnp.where(same, 1.0, 0.0)
            sel[:, zs * tok : (zs + 1) * tok] = one.astype(BF16)
            selt[zs * tok : (zs + 1) * tok, :] = one.T.astype(BF16)
            gates = gates + jnp.where(same, w.reshape(total, tok), 0.0)
        gate = jnp.broadcast_to(jnp.sum(gates, axis=1, keepdims=True), (total, tok))
        gsend[...] = gate.reshape(peers, rows, tok)
        for k in range(1, peers):
            d = lax.rem(mp + k, peers)
            remote(gsend.at[d], grecv.at[mp], gate_sem.at[0], gate_sem.at[1], pdev(d)).start()
        local(gsend.at[mp], grecv.at[mp], gate_sem.at[1]).start()

    def tick_a(t, carry):
        for h in range(NS):
            at(HA * (half - 1), nitem, t, lambda i, h=h: ag_far(i, h))
            for s in range(half - 1, 1, -1):
                at(HA * (s - 1), nitem, t, lambda i, s=s, h=h: ag_mid(i, s, h))
            at(-1, nitem, t, lambda i, h=h: first(i, h))
            if h == 0:
                @pl.when(t == HA * half - 1)
                def _():
                    build()

                at(HA * half, nitem, t, spread)

        @pl.when(t == HA * half + 1)
        def _():
            for q, (hbm, vm) in enumerate(((wg_hbm, wg), (wu_hbm, wu), (wd_hbm, wd))):
                local(vm, vm, w_sem.at[q]).wait()

        at(HA * half + YL, nitem, t, products)
        at(nch + HA * half + YL, peers, t, activate)
        at(HA * half + YL, nitem, t, ag_drain)
        return carry

    lax.fori_loop(0, nitem + HA * half + YL, tick_a, 0)

    local(grecv, grecv, gate_sem.at[1]).wait()
    local(gsend.at[pl.ds(0, peers - 1)], gsend.at[pl.ds(0, peers - 1)], gate_sem.at[0]).wait()

    @pl.loop(0, total // 16)
    def _(q):
        at_rows = pl.ds(pl.multiple_of(q * 16, 16), 16)
        hid[at_rows, :] = (
            acc[1, at_rows, :] * acc[2, at_rows, :] + acc[0, at_rows, :] * acc[3, at_rows, :]
        ).astype(BF16)
        acc[2, at_rows, :] = jnp.zeros((16, ff), F32)

    def gate_lanes():
        gl = grecv[...].reshape(total, tok)
        return jnp.concatenate([gl] * (width // tok), axis=1)

    def tangent_out(j):
        slot = lax.rem(j, STG)
        pt = jnp.dot(hid[...], wd[j], preferred_element_type=F32) * gate_lanes()
        rstg[slot] = pt.astype(BF16).reshape(peers, rows, width)
        return_send(j, slot)

    def home(j):
        combine(j, lax.rem(j, STG))
        rs_first(j)

    def finish_jv(j, h):
        jv = rs_final(j, h) + g[nch + j, mz, part(h)].astype(F32)
        jvf[j, part(h)] = jv
        ssacc[part(h)] += jv * jv
        g[j, mz, part(h)] = jv.astype(BF16)
        ag_first(j, h)

    def spread_jv(j):
        rs_drain(j)
        ag_done(j)
        dispatch(j, lax.rem(j, STG))
        dispatch_send(j, lax.rem(j, STG))

    contract_last = (((1,), (1,)), ((), ()))

    def back(j):
        dispatch_wait(j, lax.rem(j, STG))
        ag_drain(j)
        got = r[j].reshape(total, width)
        for n in range(ff // width):
            cols = slice(n * width, (n + 1) * width)
            acc[2, :, cols] += lax.dot_general(
                got, wd[j, cols, :], contract_last, preferred_element_type=F32
            )

    rl = YL
    al = rl + HB * half

    def tick_b(t, carry):
        for h in range(NS):
            at(al + HB * (half - 1), nch, t, lambda j, h=h: ag_far(j, h))
            for s in range(half - 1, 1, -1):
                at(al + HB * (s - 1), nch, t, lambda j, s=s, h=h: ag_mid(j, s, h))
            for s in range(half - 1, 1, -1):
                at(rl + HB * s, nch, t, lambda j, s=s, h=h: rs_mid(j, s, h))
            at(rl + HB, nch, t, lambda j, h=h: rs_second(j, h))
            at(al, nch, t, lambda j, h=h: finish_jv(j, h))
            if h == 0:
                at(al + HB * half, nch, t, spread_jv)
                at(0, nch, t, tangent_out)
        at(rl, nch, t, home)
        at(al + HB * half + YL, nch, t, back)
        return carry

    lax.fori_loop(0, nch + al + HB * half + YL, tick_b, 0)

    def exchange(stage, me_slot, count, dev_of):
        for k in range(1, count):
            d = lax.rem(me_slot + k, count)
            pltpu.make_async_remote_copy(
                src_ref=red.at[stage, me_slot], dst_ref=red.at[stage, me_slot],
                send_sem=red_sem.at[0, stage], recv_sem=red_sem.at[1, stage],
                device_id=dev_of(d), device_id_type=MESH,
            ).start()

    def gathered(stage, count):
        span = red.at[stage, pl.ds(0, count - 1)]
        local(span, span, red_sem.at[1, stage]).wait()
        local(span, span, red_sem.at[0, stage]).wait()
        value = red[stage, 0]
        for k in range(1, count):
            value = value + red[stage, k]
        return value

    squares = jnp.sum(jnp.sum(ssacc[...], axis=1, keepdims=True), axis=0, keepdims=True)
    red[0, mp] = jnp.broadcast_to(squares, (8, 128))
    if peers > 1:
        exchange(0, mp, peers, lambda d: {"expert": pdev(d)})

    @pl.loop(0, total // 16)
    def _(q):
        at_rows = pl.ds(pl.multiple_of(q * 16, 16), 16)
        gl = grecv[q // (rows // 16), pl.ds(pl.multiple_of(lax.rem(q, rows // 16) * 16, 16), 16), :]
        bk = acc[2, at_rows, :] * jnp.concatenate([gl] * (ff // tok), axis=1)
        gru[0, at_rows, :] = (bk * acc[1, at_rows, :]).astype(BF16)
        gru[1, at_rows, :] = (bk * acc[0, at_rows, :]).astype(BF16)

    def grad_out(j):
        slot = lax.rem(j, STG)
        pg = lax.dot_general(gru[0], wg[j], contract_last, preferred_element_type=F32)
        pg = pg + lax.dot_general(gru[1], wu[j], contract_last, preferred_element_type=F32)
        rstg[slot] = pg.astype(BF16).reshape(peers, rows, width)
        return_send(j, slot)

    def out_copy(j, slot):
        return local(ostg.at[slot], out_hbm.at[:, pl.ds(pl.multiple_of(j * width, width), width)], o_sem.at[slot])

    def finish_out(j, h):
        slot = lax.rem(j, 2)
        if h == 0:
            @pl.when(j >= 2)
            def _():
                out_copy(j - 2, slot).wait()

        mean = red[3, 0][0:1, 0:1] * (1.0 / (tok * nx * ny * nz * 2.0 * nch * width))
        scale = jnp.broadcast_to(lax.rsqrt(mean + 1e-06), (part_rows, width))
        ostg[slot, part(h)] = (rs_final(j, h) + jvf[j, part(h)]) * scale
        if h == NS - 1:
            out_copy(j, slot).start()

    dl = rl + HD * half

    def tick_d(t, carry):
        for h in range(NS):
            for s in range(half - 1, 1, -1):
                at(rl + HD * s, nch, t, lambda j, s=s, h=h: rs_mid(j, s, h))
            at(rl + HD, nch, t, lambda j, h=h: rs_second(j, h))
            if h == 0:
                at(0, nch, t, grad_out)

        @pl.when(t == 1)
        def _():
            red[1, mz] = gathered(0, peers)
            exchange(1, mz, nz, lambda d: {"expert": zdev(d)})

        at(rl, nch, t, home)

        @pl.when(t == rl + 1)
        def _():
            red[2, mx] = gathered(1, nz)
            if nx > 1:
                exchange(2, mx, nx, lambda d: {"dp": d})

        @pl.when(t == dl)
        def _():
            red[3, 0] = gathered(2, nx) if nx > 1 else red[2, 0]

        for h in range(NS):
            at(dl, nch, t, lambda j, h=h: finish_out(j, h))
        return carry

    lax.fori_loop(0, nch + dl, tick_d, 0)
    for j in range(nch):
        rs_drain(j)
    for j in range(max(0, nch - 2), nch):
        out_copy(j, j % 2).wait()


def shards(ny, nz, nx, tokens, tangent, routes, gates, w_gate, w_up, w_down):
    tok, depth = tokens.shape
    ff = w_gate.shape[2]
    width = 256
    nch = depth // width
    peers = 2 * ny
    rows = -(-(nz * CAP) // 16) * 16
    total = peers * rows
    slots = max(nz, peers, nx)
    dma = pltpu.SemaphoreType.DMA
    scratch = [
        pltpu.VMEM((nch, width, ff), BF16),
        pltpu.VMEM((nch, width, ff), BF16),
        pltpu.VMEM((nch, ff, width), BF16),
        pltpu.VMEM((2 * nch, nz, tok, width), BF16),
        pltpu.VMEM((2 * nch, peers, rows, width), BF16),
        pltpu.VMEM((total, nz * tok), BF16),
        pltpu.VMEM((nz * tok, total), BF16),
        pltpu.VMEM((4, total, ff), F32),
        pltpu.VMEM((total, ff), BF16),
        pltpu.VMEM((2, total, ff), BF16),
        pltpu.VMEM((nch, peers, rows, width), BF16),
        pltpu.VMEM((nch, nz, tok, width), BF16),
        pltpu.VMEM((nch, nz - 1, tok, width), BF16),
        pltpu.VMEM((STG, peers, rows, width), BF16),
        pltpu.VMEM((STG, peers, rows, width), BF16),
        pltpu.VMEM((nch, tok, width), F32),
        pltpu.VMEM((2, tok, width), F32),
        pltpu.VMEM((nz, 2 * peers, tok), F32),
        pltpu.VMEM((nz, 2 * peers, tok), F32),
        pltpu.VMEM((peers, rows, tok), F32),
        pltpu.VMEM((peers, rows, tok), F32),
        pltpu.VMEM((4, slots, 8, 128), F32),
        pltpu.VMEM((tok, width), F32),
        dma((2 * nch,)),
        dma((3,)),
        dma((2 * nch, nz - 1, NS)),
        dma((2 * nch,)),
        dma((2 * nch,)),
        dma((STG,)),
        dma((nch,)),
        dma((STG,)),
        dma((nch, nz - 1, NS)),
        dma((nch,)),
        dma((2,)),
        dma((2,)),
        dma((2,)),
        dma((2, 3)),
    ]
    anywhere = pl.BlockSpec(memory_space=pl.ANY)
    vmem = pl.BlockSpec(memory_space=pltpu.VMEM)
    return pl.pallas_call(
        functools.partial(body, ny, nz, nx, (tok, width, rows, nch, ff)),
        out_shape=jax.ShapeDtypeStruct((tok, depth), F32),
        in_specs=[anywhere, anywhere, vmem, vmem, anywhere, anywhere, anywhere],
        out_specs=anywhere,
        scratch_shapes=scratch,
        compiler_params=pltpu.CompilerParams(
            collective_id=0, has_side_effects=True, vmem_limit_bytes=67043328
        ),
        name="gauss_newton_moe",
    )(tokens, tangent, routes.T, gates.T, w_gate, w_up, w_down)


def build(mesh, ny, nz):
    placed = (
        P(("dp", "expert"), None),
        P(("dp", "expert"), None),
        P(("dp", "expert"), None),
        P(("dp", "expert"), None),
        P("expert", None, None),
        P("expert", None, None),
        P("expert", None, None),
    )
    return jax.shard_map(
        functools.partial(shards, ny, nz, mesh.shape["dp"]),
        mesh=mesh,
        in_specs=placed,
        out_specs=P(("dp", "expert"), None),
        check_vma=False,
    )


def solution(mesh):
    return build(mesh, 4, 8)
```

```python
import functools
import jax
import jax.numpy as jnp
from jax import lax
from jax.experimental import pallas as pl
from jax.experimental.pallas import tpu as pltpu
from jax.sharding import PartitionSpec as P

MESH = pl.DeviceIdType.MESH
F32 = jnp.float32
BF16 = jnp.bfloat16
CAP = 9
STG = 3
HA = 1
HB = 1
HD = 1
YL = 2
NS = 2


def body(
    ny, nz, nx, dims, x_hbm, v_hbm, rt_ref, gt_ref, wg_hbm, wu_hbm, wd_hbm, out_hbm,
    wg, wu, wd, g, r, sel, selt, acc, hid, gru, ret, yb, rs, stg, rstg, jvf, ostg,
    metas, metar, gsend, grecv, red, ssacc,
    load_sem, w_sem, ag_r, ag_s, y_r, y_s, rt_r, rt_s, rs_r, rs_s, o_sem, meta_sem, gate_sem, red_sem,
):
    tok, width, rows, nch, ff = dims
    peers = 2 * ny
    half = nz // 2
    nitem = 2 * nch
    total = peers * rows
    me = lax.axis_index("expert")
    mx = lax.axis_index("dp")
    my = me // (2 * nz)
    mz = lax.rem(me // 2, nz)
    mc = lax.rem(me, 2)
    mp = my * 2 + mc

    def zdev(zt):
        return my * (2 * nz) + zt * 2 + mc

    def pdev(d):
        return (d // 2) * (2 * nz) + mz * 2 + lax.rem(d, 2)

    def zoff(k):
        return lax.rem(mz + (k + nz), nz)

    right = zdev(zoff(1))
    left = zdev(zoff(-1))

    def local(src, dst, sem):
        return pltpu.make_async_copy(src, dst, sem)

    def remote(src, dst, ssem, rsem, dev):
        return pltpu.make_async_remote_copy(
            src_ref=src, dst_ref=dst, send_sem=ssem, recv_sem=rsem,
            device_id={"expert": dev}, device_id_type=MESH,
        )

    def load(i, hbm, ch):
        return local(hbm.at[:, pl.ds(ch * width, width)], g.at[i, mz], load_sem.at[i])

    for ch in range(min(2, nch)):
        load(ch, x_hbm, ch).start()

    barrier = pltpu.get_barrier_semaphore()
    for k in range(1, nz):
        pl.semaphore_signal(barrier, inc=1, device_id={"expert": zdev(zoff(k))}, device_id_type=MESH)
    for k in range(1, peers):
        pl.semaphore_signal(
            barrier, inc=1, device_id={"expert": pdev(lax.rem(mp + k, peers))}, device_id_type=MESH
        )
    for k in range(1, nx):
        pl.semaphore_signal(
            barrier, inc=1, device_id={"dp": lax.rem(mx + k, nx)}, device_id_type=MESH
        )

    pl.semaphore_wait(barrier, (nz - 1) + (peers - 1) + (nx - 1))

    part_rows = tok // NS

    def part(h):
        return pl.ds(h * part_rows, part_rows)

    def ag_send(i, slot, h, zs, dev):
        piece = g.at[i, zs, part(h)]
        remote(piece, piece, ag_s.at[i], ag_r.at[i, slot, h], dev).start()

    def ag_wait(i, slot, h):
        piece = g.at[i, mz, part(h)]
        remote(piece, piece, ag_s.at[i], ag_r.at[i, slot, h], right).wait_recv()

    def ag_first(i, h):
        ag_send(i, 0, h, mz, right)
        ag_send(i, 1, h, mz, left)

    def ag_mid(i, s, h):
        ag_wait(i, 2 * (s - 2), h)
        ag_send(i, 2 * (s - 1), h, zoff(-(s - 1)), right)
        ag_wait(i, 2 * (s - 2) + 1, h)
        ag_send(i, 2 * (s - 1) + 1, h, zoff(s - 1), left)

    def ag_far(i, h):
        par = lax.rem(i, 2)
        ag_wait(i, 2 * (half - 2), h)
        ag_wait(i, 2 * (half - 2) + 1, h)
        zs = jnp.where(par == 0, zoff(-(half - 1)), zoff(half - 1))
        ag_send(i, 2 * half - 2, h, zs, jnp.where(par == 0, right, left))

    def ag_done(i):
        for h in range(NS):
            ag_wait(i, 2 * half - 2, h)

    def ag_drain(i):
        local(g.at[i, pl.ds(0, nz - 1)], g.at[i, pl.ds(0, nz - 1)], ag_s.at[i]).wait()

    def first(i, h):
        if h == 0:
            load(i, x_hbm, 0).wait()
        ag_first(i, h)

    for h in range(NS):
        first(0, h)

    for ch in range(2, nch):
        load(ch, x_hbm, ch).start()
    for ch in range(nch):
        load(nch + ch, v_hbm, ch).start()
    for ch in range(nch):
        local(wg_hbm.at[0, pl.ds(ch * width, width), :], wg.at[ch], w_sem.at[0]).start()
        local(wu_hbm.at[0, pl.ds(ch * width, width), :], wu.at[ch], w_sem.at[1]).start()
    for ch in range(nch):
        local(wd_hbm.at[0, :, pl.ds(ch * width, width)], wd.at[ch], w_sem.at[2]).start()

    pshift = peers.bit_length() - 1
    row = lax.broadcasted_iota(jnp.int32, (nz * peers, tok), 0)
    zrow = lax.shift_right_logical(row, pshift)
    drow = jnp.bitwise_and(row, peers - 1)
    expert = lax.shift_right_logical(drow, 1) * (2 * nz) + zrow * 2 + jnp.bitwise_and(drow, 1)
    named = jnp.zeros((nz * peers, tok), F32)
    weight = jnp.zeros((nz * peers, tok), F32)
    for k in range(rt_ref.shape[0]):
        hit = jnp.broadcast_to(rt_ref[k : k + 1, :], expert.shape) == expert
        named = named + jnp.where(hit, 1.0, 0.0)
        weight = weight + jnp.where(hit, jnp.broadcast_to(gt_ref[k : k + 1, :], expert.shape), 0.0)
    earlier = lax.broadcasted_iota(jnp.int32, (tok, tok), 0) < lax.broadcasted_iota(
        jnp.int32, (tok, tok), 1
    )
    rank = jnp.dot(
        named.astype(BF16), jnp.where(earlier, 1.0, 0.0).astype(BF16), preferred_element_type=F32
    )
    base = (mz * CAP).astype(F32)
    code = jnp.where(named > 0.5, rank + base, -1.0)
    for zt in range(nz):
        metas[zt, 0:peers, :] = code[zt * peers : (zt + 1) * peers]
        metas[zt, peers : 2 * peers, :] = weight[zt * peers : (zt + 1) * peers]
    metar[mz] = metas[mz]

    @pl.loop(0, total // 16)
    def _(q):
        for m in range(4):
            acc[m, pl.ds(pl.multiple_of(q * 16, 16), 16), :] = jnp.zeros((16, ff), F32)

    ssacc[...] = jnp.zeros(ssacc.shape, F32)
    for k in range(1, nz):
        zt = zoff(k)
        remote(metas.at[zt], metar.at[mz], meta_sem.at[0], meta_sem.at[1], zdev(zt)).start()

    def dispatch(i, slot):
        tokens = g[i].reshape(nz * tok, width)
        picked = jnp.dot(sel[...], tokens, preferred_element_type=F32)
        stg[slot] = picked.astype(BF16).reshape(peers, rows, width)

    def dispatch_send(i, slot):
        for k in range(1, peers):
            d = lax.rem(mp + k, peers)
            remote(stg.at[slot, d], r.at[i, mp], y_s.at[slot], y_r.at[i], pdev(d)).start()
        local(stg.at[slot, mp], r.at[i, mp], y_r.at[i]).start()

    def dispatch_wait(i, slot):
        local(r.at[i], r.at[i], y_r.at[i]).wait()
        local(
            stg.at[slot, pl.ds(0, peers - 1)], stg.at[slot, pl.ds(0, peers - 1)], y_s.at[slot]
        ).wait()

    def return_send(j, slot):
        for k in range(1, peers):
            d = lax.rem(mp + k, peers)
            remote(rstg.at[slot, d], ret.at[j, mp], rt_s.at[slot], rt_r.at[j], pdev(d)).start()
        local(rstg.at[slot, mp], ret.at[j, mp], rt_r.at[j]).start()

    def combine(j, slot):
        local(ret.at[j], ret.at[j], rt_r.at[j]).wait()
        local(
            rstg.at[slot, pl.ds(0, peers - 1)], rstg.at[slot, pl.ds(0, peers - 1)], rt_s.at[slot]
        ).wait()
        back_rows = ret[j].reshape(total, width)
        sums = jnp.dot(selt[...], back_rows, preferred_element_type=F32)
        yb[j] = sums.astype(BF16).reshape(nz, tok, width)

    far = 2 * (half - 1)

    def rs_send(j, src, slot, h, dev):
        remote(src, rs.at[j, slot, part(h)], rs_s.at[j], rs_r.at[j, slot, h], dev).start()

    def rs_wait(j, slot, h):
        piece = rs.at[j, slot, part(h)]
        remote(piece, piece, rs_s.at[j], rs_r.at[j, slot, h], right).wait_recv()

    def rs_add(j, slot, h, zd):
        rs[j, slot, part(h)] = (
            rs[j, slot, part(h)].astype(F32) + yb[j, zd, part(h)].astype(F32)
        ).astype(BF16)

    def rs_first(j):
        par = lax.rem(j, 2)
        zd = jnp.where(par == 0, zoff(-(half - 1)), zoff(half - 1))
        for h in range(NS):
            rs_send(j, yb.at[j, zoff(half), part(h)], far, h, jnp.where(par == 0, right, left))
            rs_send(j, yb.at[j, zd, part(h)], 1 - par, h, jnp.where(par == 0, left, right))

    def rs_second(j, h):
        par = lax.rem(j, 2)
        rs_wait(j, far, h)
        rs_add(j, far, h, jnp.where(par == 0, zoff(half - 1), zoff(-(half - 1))))
        rs_send(j, rs.at[j, far, part(h)], par, h, jnp.where(par == 0, right, left))

    def rs_mid(j, s, h):
        up = 2 * (s - 2)
        rs_wait(j, up, h)
        rs_add(j, up, h, zoff(half - s))
        rs_send(j, rs.at[j, up, part(h)], up + 2, h, right)
        rs_wait(j, up + 1, h)
        rs_add(j, up + 1, h, zoff(-(half - s)))
        rs_send(j, rs.at[j, up + 1, part(h)], up + 3, h, left)

    def rs_final(j, h):
        rs_wait(j, far - 2, h)
        rs_wait(j, far - 1, h)
        return (
            rs[j, far - 2, part(h)].astype(F32)
            + rs[j, far - 1, part(h)].astype(F32)
            + yb[j, mz, part(h)].astype(F32)
        )

    def rs_drain(j):
        local(rs.at[j], rs.at[j], rs_s.at[j]).wait()

    def at(lag, count, tick, fn):
        i = tick - lag

        @pl.when((i >= 0) & (i < count))
        def _():
            fn(i)

    def products(i):
        dispatch_wait(i, lax.rem(i, STG))
        ch = lax.rem(i, nch)
        m = (i // nch) * 2
        got = r[i].reshape(total, width)
        for n in range(ff // width):
            cols = slice(n * width, (n + 1) * width)
            acc[m, :, cols] += jnp.dot(got, wg[ch, :, cols], preferred_element_type=F32)
            acc[m + 1, :, cols] += jnp.dot(got, wu[ch, :, cols], preferred_element_type=F32)

    def activate(q):
        for k in range(rows // 16):
            at_rows = pl.ds(pl.multiple_of(q * rows + k * 16, 16), 16)
            a = acc[0, at_rows, :]
            s = jax.nn.sigmoid(a)
            acc[0, at_rows, :] = a * s
            acc[1, at_rows, :] = s * (1.0 + a * (1.0 - s)) * acc[1, at_rows, :]

    def spread(i):
        ag_done(i)
        dispatch(i, lax.rem(i, STG))
        dispatch_send(i, lax.rem(i, STG))

    def build():
        local(metar.at[pl.ds(0, nz - 1)], metar.at[pl.ds(0, nz - 1)], meta_sem.at[1]).wait()
        local(metas.at[pl.ds(0, nz - 1)], metas.at[pl.ds(0, nz - 1)], meta_sem.at[0]).wait()
        slot_id = lax.broadcasted_iota(jnp.int32, (peers, rows, tok), 1).astype(F32)
        slot_id = slot_id.reshape(total, tok)
        gates = jnp.zeros((total, tok), F32)
        for zs in range(nz):
            q = jnp.broadcast_to(metar[zs, 0:peers, :][:, None, :], (peers, rows, tok))
            w = jnp.broadcast_to(metar[zs, peers : 2 * peers, :][:, None, :], (peers, rows, tok))
            same = q.reshape(total, tok) == slot_id
            one = jnp.where(same, 1.0, 0.0)
            sel[:, zs * tok : (zs + 1) * tok] = one.astype(BF16)
            selt[zs * tok : (zs + 1) * tok, :] = one.T.astype(BF16)
            gates = gates + jnp.where(same, w.reshape(total, tok), 0.0)
        gate = jnp.broadcast_to(jnp.sum(gates, axis=1, keepdims=True), (total, tok))
        gsend[...] = gate.reshape(peers, rows, tok)
        for k in range(1, peers):
            d = lax.rem(mp + k, peers)
            remote(gsend.at[d], grecv.at[mp], gate_sem.at[0], gate_sem.at[1], pdev(d)).start()
        local(gsend.at[mp], grecv.at[mp], gate_sem.at[1]).start()

    def tick_a(t, carry):
        for h in range(NS):
            at(HA * (half - 1), nitem, t, lambda i, h=h: ag_far(i, h))
            for s in range(half - 1, 1, -1):
                at(HA * (s - 1), nitem, t, lambda i, s=s, h=h: ag_mid(i, s, h))
            at(-1, nitem, t, lambda i, h=h: first(i, h))
            if h == 0:
                @pl.when(t == HA * half - 1)
                def _():
                    build()

                at(HA * half, nitem, t, spread)

        @pl.when(t == HA * half + 1)
        def _():
            for q, (hbm, vm) in enumerate(((wg_hbm, wg), (wu_hbm, wu), (wd_hbm, wd))):
                local(vm, vm, w_sem.at[q]).wait()

        at(HA * half + YL, nitem, t, products)
        at(nch + HA * half + YL, peers, t, activate)
        at(HA * half + YL, nitem, t, ag_drain)
        return carry

    lax.fori_loop(0, nitem + HA * half + YL, tick_a, 0)

    local(grecv, grecv, gate_sem.at[1]).wait()
    local(gsend.at[pl.ds(0, peers - 1)], gsend.at[pl.ds(0, peers - 1)], gate_sem.at[0]).wait()

    @pl.loop(0, total // 16)
    def _(q):
        at_rows = pl.ds(pl.multiple_of(q * 16, 16), 16)
        hid[at_rows, :] = (
            acc[1, at_rows, :] * acc[2, at_rows, :] + acc[0, at_rows, :] * acc[3, at_rows, :]
        ).astype(BF16)
        acc[2, at_rows, :] = jnp.zeros((16, ff), F32)

    def gate_lanes():
        gl = grecv[...].reshape(total, tok)
        return jnp.concatenate([gl] * (width // tok), axis=1)

    def tangent_out(j):
        slot = lax.rem(j, STG)
        pt = jnp.dot(hid[...], wd[j], preferred_element_type=F32) * gate_lanes()
        rstg[slot] = pt.astype(BF16).reshape(peers, rows, width)
        return_send(j, slot)

    def home(j):
        combine(j, lax.rem(j, STG))
        rs_first(j)

    def finish_jv(j, h):
        jv = rs_final(j, h) + g[nch + j, mz, part(h)].astype(F32)
        jvf[j, part(h)] = jv
        ssacc[part(h)] += jv * jv
        g[j, mz, part(h)] = jv.astype(BF16)
        ag_first(j, h)

    def spread_jv(j):
        rs_drain(j)
        ag_done(j)
        dispatch(j, lax.rem(j, STG))
        dispatch_send(j, lax.rem(j, STG))

    contract_last = (((1,), (1,)), ((), ()))

    def back(j):
        dispatch_wait(j, lax.rem(j, STG))
        ag_drain(j)
        got = r[j].reshape(total, width)
        for n in range(ff // width):
            cols = slice(n * width, (n + 1) * width)
            acc[2, :, cols] += lax.dot_general(
                got, wd[j, cols, :], contract_last, preferred_element_type=F32
            )

    rl = YL
    al = rl + HB * half

    def tick_b(t, carry):
        for h in range(NS):
            at(al + HB * (half - 1), nch, t, lambda j, h=h: ag_far(j, h))
            for s in range(half - 1, 1, -1):
                at(al + HB * (s - 1), nch, t, lambda j, s=s, h=h: ag_mid(j, s, h))
            for s in range(half - 1, 1, -1):
                at(rl + HB * s, nch, t, lambda j, s=s, h=h: rs_mid(j, s, h))
            at(rl + HB, nch, t, lambda j, h=h: rs_second(j, h))
            at(al, nch, t, lambda j, h=h: finish_jv(j, h))
            if h == 0:
                at(al + HB * half, nch, t, spread_jv)
                at(rl, nch, t, home)
        at(0, nch, t, tangent_out)
        at(al + HB * half + YL, nch, t, back)
        return carry

    lax.fori_loop(0, nch + al + HB * half + YL, tick_b, 0)

    def exchange(stage, me_slot, count, dev_of):
        for k in range(1, count):
            d = lax.rem(me_slot + k, count)
            pltpu.make_async_remote_copy(
                src_ref=red.at[stage, me_slot], dst_ref=red.at[stage, me_slot],
                send_sem=red_sem.at[0, stage], recv_sem=red_sem.at[1, stage],
                device_id=dev_of(d), device_id_type=MESH,
            ).start()

    def gathered(stage, count):
        span = red.at[stage, pl.ds(0, count - 1)]
        local(span, span, red_sem.at[1, stage]).wait()
        local(span, span, red_sem.at[0, stage]).wait()
        value = red[stage, 0]
        for k in range(1, count):
            value = value + red[stage, k]
        return value

    squares = jnp.sum(jnp.sum(ssacc[...], axis=1, keepdims=True), axis=0, keepdims=True)
    red[0, mp] = jnp.broadcast_to(squares, (8, 128))
    if peers > 1:
        exchange(0, mp, peers, lambda d: {"expert": pdev(d)})

    @pl.loop(0, total // 16)
    def _(q):
        at_rows = pl.ds(pl.multiple_of(q * 16, 16), 16)
        gl = grecv[q // (rows // 16), pl.ds(pl.multiple_of(lax.rem(q, rows // 16) * 16, 16), 16), :]
        bk = acc[2, at_rows, :] * jnp.concatenate([gl] * (ff // tok), axis=1)
        gru[0, at_rows, :] = (bk * acc[1, at_rows, :]).astype(BF16)
        gru[1, at_rows, :] = (bk * acc[0, at_rows, :]).astype(BF16)

    def grad_out(j):
        slot = lax.rem(j, STG)
        pg = lax.dot_general(gru[0], wg[j], contract_last, preferred_element_type=F32)
        pg = pg + lax.dot_general(gru[1], wu[j], contract_last, preferred_element_type=F32)
        rstg[slot] = pg.astype(BF16).reshape(peers, rows, width)
        return_send(j, slot)

    def out_copy(j, slot):
        return local(ostg.at[slot], out_hbm.at[:, pl.ds(pl.multiple_of(j * width, width), width)], o_sem.at[slot])

    def finish_out(j, h):
        slot = lax.rem(j, 2)
        if h == 0:
            @pl.when(j >= 2)
            def _():
                out_copy(j - 2, slot).wait()

        mean = red[3, 0][0:1, 0:1] * (1.0 / (tok * nx * ny * nz * 2.0 * nch * width))
        scale = jnp.broadcast_to(lax.rsqrt(mean + 1e-06), (part_rows, width))
        ostg[slot, part(h)] = (rs_final(j, h) + jvf[j, part(h)]) * scale
        if h == NS - 1:
            out_copy(j, slot).start()

    dl = rl + HD * half

    def tick_d(t, carry):
        for h in range(NS):
            for s in range(half - 1, 1, -1):
                at(rl + HD * s, nch, t, lambda j, s=s, h=h: rs_mid(j, s, h))
            at(rl + HD, nch, t, lambda j, h=h: rs_second(j, h))
            if h == 0:
                at(rl, nch, t, home)
        at(0, nch, t, grad_out)

        @pl.when(t == 1)
        def _():
            red[1, mz] = gathered(0, peers)
            exchange(1, mz, nz, lambda d: {"expert": zdev(d)})

        @pl.when(t == rl + 1)
        def _():
            red[2, mx] = gathered(1, nz)
            if nx > 1:
                exchange(2, mx, nx, lambda d: {"dp": d})

        @pl.when(t == dl)
        def _():
            red[3, 0] = gathered(2, nx) if nx > 1 else red[2, 0]

        for h in range(NS):
            at(dl, nch, t, lambda j, h=h: finish_out(j, h))
        return carry

    lax.fori_loop(0, nch + dl, tick_d, 0)
    for j in range(nch):
        rs_drain(j)
    for j in range(max(0, nch - 2), nch):
        out_copy(j, j % 2).wait()


def shards(ny, nz, nx, tokens, tangent, routes, gates, w_gate, w_up, w_down):
    tok, depth = tokens.shape
    ff = w_gate.shape[2]
    width = 256
    nch = depth // width
    peers = 2 * ny
    rows = -(-(nz * CAP) // 16) * 16
    total = peers * rows
    slots = max(nz, peers, nx)
    dma = pltpu.SemaphoreType.DMA
    scratch = [
        pltpu.VMEM((nch, width, ff), BF16),
        pltpu.VMEM((nch, width, ff), BF16),
        pltpu.VMEM((nch, ff, width), BF16),
        pltpu.VMEM((2 * nch, nz, tok, width), BF16),
        pltpu.VMEM((2 * nch, peers, rows, width), BF16),
        pltpu.VMEM((total, nz * tok), BF16),
        pltpu.VMEM((nz * tok, total), BF16),
        pltpu.VMEM((4, total, ff), F32),
        pltpu.VMEM((total, ff), BF16),
        pltpu.VMEM((2, total, ff), BF16),
        pltpu.VMEM((nch, peers, rows, width), BF16),
        pltpu.VMEM((nch, nz, tok, width), BF16),
        pltpu.VMEM((nch, nz - 1, tok, width), BF16),
        pltpu.VMEM((STG, peers, rows, width), BF16),
        pltpu.VMEM((STG, peers, rows, width), BF16),
        pltpu.VMEM((nch, tok, width), F32),
        pltpu.VMEM((2, tok, width), F32),
        pltpu.VMEM((nz, 2 * peers, tok), F32),
        pltpu.VMEM((nz, 2 * peers, tok), F32),
        pltpu.VMEM((peers, rows, tok), F32),
        pltpu.VMEM((peers, rows, tok), F32),
        pltpu.VMEM((4, slots, 8, 128), F32),
        pltpu.VMEM((tok, width), F32),
        dma((2 * nch,)),
        dma((3,)),
        dma((2 * nch, nz - 1, NS)),
        dma((2 * nch,)),
        dma((2 * nch,)),
        dma((STG,)),
        dma((nch,)),
        dma((STG,)),
        dma((nch, nz - 1, NS)),
        dma((nch,)),
        dma((2,)),
        dma((2,)),
        dma((2,)),
        dma((2, 3)),
    ]
    anywhere = pl.BlockSpec(memory_space=pl.ANY)
    vmem = pl.BlockSpec(memory_space=pltpu.VMEM)
    return pl.pallas_call(
        functools.partial(body, ny, nz, nx, (tok, width, rows, nch, ff)),
        out_shape=jax.ShapeDtypeStruct((tok, depth), F32),
        in_specs=[anywhere, anywhere, vmem, vmem, anywhere, anywhere, anywhere],
        out_specs=anywhere,
        scratch_shapes=scratch,
        compiler_params=pltpu.CompilerParams(
            collective_id=0, has_side_effects=True, vmem_limit_bytes=67043328
        ),
        name="gauss_newton_moe",
    )(tokens, tangent, routes.T, gates.T, w_gate, w_up, w_down)


def build(mesh, ny, nz):
    placed = (
        P(("dp", "expert"), None),
        P(("dp", "expert"), None),
        P(("dp", "expert"), None),
        P(("dp", "expert"), None),
        P("expert", None, None),
        P("expert", None, None),
        P("expert", None, None),
    )
    return jax.shard_map(
        functools.partial(shards, ny, nz, mesh.shape["dp"]),
        mesh=mesh,
        in_specs=placed,
        out_specs=P(("dp", "expert"), None),
        check_vma=False,
    )


def solution(mesh):
    return build(mesh, 4, 8)
```

```python
import functools
import jax
import jax.numpy as jnp
from jax import lax
from jax.experimental import pallas as pl
from jax.experimental.pallas import tpu as pltpu
from jax.sharding import PartitionSpec as P

MESH = pl.DeviceIdType.MESH
F32 = jnp.float32
BF16 = jnp.bfloat16
CAP = 9
STG = 3
HA = 1
HB = 1
HD = 1
YL = 2
NS = 2


def body(
    ny, nz, nx, dims, x_hbm, v_hbm, rt_ref, gt_ref, wg_hbm, wu_hbm, wd_hbm, out_hbm,
    wg, wu, wd, g, r, sel, selt, acc, hid, gru, ret, yb, rs, stg, rstg, jvf, ostg,
    metas, metar, gsend, grecv, red, ssacc,
    load_sem, w_sem, ag_r, ag_s, y_r, y_s, rt_r, rt_s, rs_r, rs_s, o_sem, meta_sem, gate_sem, red_sem,
):
    tok, width, rows, nch, ff = dims
    peers = 2 * ny
    half = nz // 2
    nitem = 2 * nch
    total = peers * rows
    me = lax.axis_index("expert")
    mx = lax.axis_index("dp")
    my = me // (2 * nz)
    mz = lax.rem(me // 2, nz)
    mc = lax.rem(me, 2)
    mp = my * 2 + mc

    def zdev(zt):
        return my * (2 * nz) + zt * 2 + mc

    def pdev(d):
        return (d // 2) * (2 * nz) + mz * 2 + lax.rem(d, 2)

    def zoff(k):
        return lax.rem(mz + (k + nz), nz)

    right = zdev(zoff(1))
    left = zdev(zoff(-1))

    def local(src, dst, sem):
        return pltpu.make_async_copy(src, dst, sem)

    def remote(src, dst, ssem, rsem, dev):
        return pltpu.make_async_remote_copy(
            src_ref=src, dst_ref=dst, send_sem=ssem, recv_sem=rsem,
            device_id={"expert": dev}, device_id_type=MESH,
        )

    def load(i, hbm, ch):
        return local(hbm.at[:, pl.ds(ch * width, width)], g.at[i, mz], load_sem.at[i])

    for ch in range(min(2, nch)):
        load(ch, x_hbm, ch).start()

    barrier = pltpu.get_barrier_semaphore()
    for k in range(1, nz):
        pl.semaphore_signal(barrier, inc=1, device_id={"expert": zdev(zoff(k))}, device_id_type=MESH)
    for k in range(1, peers):
        pl.semaphore_signal(
            barrier, inc=1, device_id={"expert": pdev(lax.rem(mp + k, peers))}, device_id_type=MESH
        )
    for k in range(1, nx):
        pl.semaphore_signal(
            barrier, inc=1, device_id={"dp": lax.rem(mx + k, nx)}, device_id_type=MESH
        )

    pl.semaphore_wait(barrier, (nz - 1) + (peers - 1) + (nx - 1))

    part_rows = tok // NS

    def part(h):
        return pl.ds(h * part_rows, part_rows)

    def ag_send(i, slot, h, zs, dev):
        piece = g.at[i, zs, part(h)]
        remote(piece, piece, ag_s.at[i], ag_r.at[i, slot, h], dev).start()

    def ag_wait(i, slot, h):
        piece = g.at[i, mz, part(h)]
        remote(piece, piece, ag_s.at[i], ag_r.at[i, slot, h], right).wait_recv()

    def ag_first(i, h):
        ag_send(i, 0, h, mz, right)
        ag_send(i, 1, h, mz, left)

    def ag_mid(i, s, h):
        ag_wait(i, 2 * (s - 2), h)
        ag_send(i, 2 * (s - 1), h, zoff(-(s - 1)), right)
        ag_wait(i, 2 * (s - 2) + 1, h)
        ag_send(i, 2 * (s - 1) + 1, h, zoff(s - 1), left)

    def ag_far(i, h):
        par = lax.rem(i, 2)
        ag_wait(i, 2 * (half - 2), h)
        ag_wait(i, 2 * (half - 2) + 1, h)
        zs = jnp.where(par == 0, zoff(-(half - 1)), zoff(half - 1))
        ag_send(i, 2 * half - 2, h, zs, jnp.where(par == 0, right, left))

    def ag_done(i):
        for h in range(NS):
            ag_wait(i, 2 * half - 2, h)

    def ag_drain(i):
        local(g.at[i, pl.ds(0, nz - 1)], g.at[i, pl.ds(0, nz - 1)], ag_s.at[i]).wait()

    def first(i, h):
        if h == 0:
            load(i, x_hbm, 0).wait()
        ag_first(i, h)

    for h in range(NS):
        first(0, h)

    for ch in range(2, nch):
        load(ch, x_hbm, ch).start()
    for ch in range(nch):
        load(nch + ch, v_hbm, ch).start()
    for ch in range(nch):
        local(wg_hbm.at[0, pl.ds(ch * width, width), :], wg.at[ch], w_sem.at[0]).start()
        local(wu_hbm.at[0, pl.ds(ch * width, width), :], wu.at[ch], w_sem.at[1]).start()
    for ch in range(nch):
        local(wd_hbm.at[0, :, pl.ds(ch * width, width)], wd.at[ch], w_sem.at[2]).start()

    pshift = peers.bit_length() - 1
    row = lax.broadcasted_iota(jnp.int32, (nz * peers, tok), 0)
    zrow = lax.shift_right_logical(row, pshift)
    drow = jnp.bitwise_and(row, peers - 1)
    expert = lax.shift_right_logical(drow, 1) * (2 * nz) + zrow * 2 + jnp.bitwise_and(drow, 1)
    named = jnp.zeros((nz * peers, tok), F32)
    weight = jnp.zeros((nz * peers, tok), F32)
    for k in range(rt_ref.shape[0]):
        hit = jnp.broadcast_to(rt_ref[k : k + 1, :], expert.shape) == expert
        named = named + jnp.where(hit, 1.0, 0.0)
        weight = weight + jnp.where(hit, jnp.broadcast_to(gt_ref[k : k + 1, :], expert.shape), 0.0)
    earlier = lax.broadcasted_iota(jnp.int32, (tok, tok), 0) < lax.broadcasted_iota(
        jnp.int32, (tok, tok), 1
    )
    rank = jnp.dot(
        named.astype(BF16), jnp.where(earlier, 1.0, 0.0).astype(BF16), preferred_element_type=F32
    )
    base = (mz * CAP).astype(F32)
    code = jnp.where(named > 0.5, rank + base, -1.0)
    for zt in range(nz):
        metas[zt, 0:peers, :] = code[zt * peers : (zt + 1) * peers]
        metas[zt, peers : 2 * peers, :] = weight[zt * peers : (zt + 1) * peers]
    metar[mz] = metas[mz]

    @pl.loop(0, total // 16)
    def _(q):
        for m in range(4):
            acc[m, pl.ds(pl.multiple_of(q * 16, 16), 16), :] = jnp.zeros((16, ff), F32)

    ssacc[...] = jnp.zeros(ssacc.shape, F32)
    for k in range(1, nz):
        zt = zoff(k)
        remote(metas.at[zt], metar.at[mz], meta_sem.at[0], meta_sem.at[1], zdev(zt)).start()

    far_first = sorted(
        [(dy, dc) for dy in range(ny) for dc in range(2) if (dy, dc) != (0, 0)],
        key=lambda p: (-min(p[0], ny - p[0]), p[1], p[0]),
    )

    def dispatch(i, slot):
        tokens = g[i].reshape(nz * tok, width)
        picked = jnp.dot(sel[...], tokens, preferred_element_type=F32)
        stg[slot] = picked.astype(BF16).reshape(peers, rows, width)

    def dispatch_send(i, slot):
        for dy, dc in far_first:
            d = lax.rem(my + dy, ny) * 2 + lax.rem(mc + dc, 2)
            remote(stg.at[slot, d], r.at[i, mp], y_s.at[slot], y_r.at[i], pdev(d)).start()
        local(stg.at[slot, mp], r.at[i, mp], y_r.at[i]).start()

    def dispatch_wait(i, slot):
        local(r.at[i], r.at[i], y_r.at[i]).wait()
        local(
            stg.at[slot, pl.ds(0, peers - 1)], stg.at[slot, pl.ds(0, peers - 1)], y_s.at[slot]
        ).wait()

    def return_send(j, slot):
        for dy, dc in far_first:
            d = lax.rem(my + dy, ny) * 2 + lax.rem(mc + dc, 2)
            remote(rstg.at[slot, d], ret.at[j, mp], rt_s.at[slot], rt_r.at[j], pdev(d)).start()
        local(rstg.at[slot, mp], ret.at[j, mp], rt_r.at[j]).start()

    def combine(j, slot):
        local(ret.at[j], ret.at[j], rt_r.at[j]).wait()
        local(
            rstg.at[slot, pl.ds(0, peers - 1)], rstg.at[slot, pl.ds(0, peers - 1)], rt_s.at[slot]
        ).wait()
        back_rows = ret[j].reshape(total, width)
        sums = jnp.dot(selt[...], back_rows, preferred_element_type=F32)
        yb[j] = sums.astype(BF16).reshape(nz, tok, width)

    far = 2 * (half - 1)

    def rs_send(j, src, slot, h, dev):
        remote(src, rs.at[j, slot, part(h)], rs_s.at[j], rs_r.at[j, slot, h], dev).start()

    def rs_wait(j, slot, h):
        piece = rs.at[j, slot, part(h)]
        remote(piece, piece, rs_s.at[j], rs_r.at[j, slot, h], right).wait_recv()

    def rs_add(j, slot, h, zd):
        rs[j, slot, part(h)] = (
            rs[j, slot, part(h)].astype(F32) + yb[j, zd, part(h)].astype(F32)
        ).astype(BF16)

    def rs_first(j):
        par = lax.rem(j, 2)
        zd = jnp.where(par == 0, zoff(-(half - 1)), zoff(half - 1))
        for h in range(NS):
            rs_send(j, yb.at[j, zoff(half), part(h)], far, h, jnp.where(par == 0, right, left))
            rs_send(j, yb.at[j, zd, part(h)], 1 - par, h, jnp.where(par == 0, left, right))

    def rs_second(j, h):
        par = lax.rem(j, 2)
        rs_wait(j, far, h)
        rs_add(j, far, h, jnp.where(par == 0, zoff(half - 1), zoff(-(half - 1))))
        rs_send(j, rs.at[j, far, part(h)], par, h, jnp.where(par == 0, right, left))

    def rs_mid(j, s, h):
        up = 2 * (s - 2)
        rs_wait(j, up, h)
        rs_add(j, up, h, zoff(half - s))
        rs_send(j, rs.at[j, up, part(h)], up + 2, h, right)
        rs_wait(j, up + 1, h)
        rs_add(j, up + 1, h, zoff(-(half - s)))
        rs_send(j, rs.at[j, up + 1, part(h)], up + 3, h, left)

    def rs_final(j, h):
        rs_wait(j, far - 2, h)
        rs_wait(j, far - 1, h)
        return (
            rs[j, far - 2, part(h)].astype(F32)
            + rs[j, far - 1, part(h)].astype(F32)
            + yb[j, mz, part(h)].astype(F32)
        )

    def rs_drain(j):
        local(rs.at[j], rs.at[j], rs_s.at[j]).wait()

    def at(lag, count, tick, fn):
        i = tick - lag

        @pl.when((i >= 0) & (i < count))
        def _():
            fn(i)

    def products(i):
        dispatch_wait(i, lax.rem(i, STG))
        ch = lax.rem(i, nch)
        m = (i // nch) * 2
        got = r[i].reshape(total, width)
        for n in range(ff // width):
            cols = slice(n * width, (n + 1) * width)
            acc[m, :, cols] += jnp.dot(got, wg[ch, :, cols], preferred_element_type=F32)
            acc[m + 1, :, cols] += jnp.dot(got, wu[ch, :, cols], preferred_element_type=F32)

    def activate(q):
        for k in range(rows // 16):
            at_rows = pl.ds(pl.multiple_of(q * rows + k * 16, 16), 16)
            a = acc[0, at_rows, :]
            s = jax.nn.sigmoid(a)
            acc[0, at_rows, :] = a * s
            acc[1, at_rows, :] = s * (1.0 + a * (1.0 - s)) * acc[1, at_rows, :]

    def spread(i):
        ag_done(i)
        dispatch(i, lax.rem(i, STG))
        dispatch_send(i, lax.rem(i, STG))

    def build():
        local(metar.at[pl.ds(0, nz - 1)], metar.at[pl.ds(0, nz - 1)], meta_sem.at[1]).wait()
        local(metas.at[pl.ds(0, nz - 1)], metas.at[pl.ds(0, nz - 1)], meta_sem.at[0]).wait()
        slot_id = lax.broadcasted_iota(jnp.int32, (peers, rows, tok), 1).astype(F32)
        slot_id = slot_id.reshape(total, tok)
        gates = jnp.zeros((total, tok), F32)
        for zs in range(nz):
            q = jnp.broadcast_to(metar[zs, 0:peers, :][:, None, :], (peers, rows, tok))
            w = jnp.broadcast_to(metar[zs, peers : 2 * peers, :][:, None, :], (peers, rows, tok))
            same = q.reshape(total, tok) == slot_id
            one = jnp.where(same, 1.0, 0.0)
            sel[:, zs * tok : (zs + 1) * tok] = one.astype(BF16)
            selt[zs * tok : (zs + 1) * tok, :] = one.T.astype(BF16)
            gates = gates + jnp.where(same, w.reshape(total, tok), 0.0)
        gate = jnp.broadcast_to(jnp.sum(gates, axis=1, keepdims=True), (total, tok))
        gsend[...] = gate.reshape(peers, rows, tok)
        for k in range(1, peers):
            d = lax.rem(mp + k, peers)
            remote(gsend.at[d], grecv.at[mp], gate_sem.at[0], gate_sem.at[1], pdev(d)).start()
        local(gsend.at[mp], grecv.at[mp], gate_sem.at[1]).start()

    def tick_a(t, carry):
        for h in range(NS):
            at(HA * (half - 1), nitem, t, lambda i, h=h: ag_far(i, h))
            for s in range(half - 1, 1, -1):
                at(HA * (s - 1), nitem, t, lambda i, s=s, h=h: ag_mid(i, s, h))
            at(-1, nitem, t, lambda i, h=h: first(i, h))
            if h == 0:
                @pl.when(t == HA * half - 1)
                def _():
                    build()

                at(HA * half, nitem, t, spread)

        @pl.when(t == HA * half + 1)
        def _():
            for q, (hbm, vm) in enumerate(((wg_hbm, wg), (wu_hbm, wu), (wd_hbm, wd))):
                local(vm, vm, w_sem.at[q]).wait()

        at(HA * half + YL, nitem, t, products)
        at(nch + HA * half + YL, peers, t, activate)
        at(HA * half + YL, nitem, t, ag_drain)
        return carry

    lax.fori_loop(0, nitem + HA * half + YL, tick_a, 0)

    local(grecv, grecv, gate_sem.at[1]).wait()
    local(gsend.at[pl.ds(0, peers - 1)], gsend.at[pl.ds(0, peers - 1)], gate_sem.at[0]).wait()

    @pl.loop(0, total // 16)
    def _(q):
        at_rows = pl.ds(pl.multiple_of(q * 16, 16), 16)
        hid[at_rows, :] = (
            acc[1, at_rows, :] * acc[2, at_rows, :] + acc[0, at_rows, :] * acc[3, at_rows, :]
        ).astype(BF16)
        acc[2, at_rows, :] = jnp.zeros((16, ff), F32)

    def gate_lanes():
        gl = grecv[...].reshape(total, tok)
        return jnp.concatenate([gl] * (width // tok), axis=1)

    def tangent_out(j):
        slot = lax.rem(j, STG)
        pt = jnp.dot(hid[...], wd[j], preferred_element_type=F32) * gate_lanes()
        rstg[slot] = pt.astype(BF16).reshape(peers, rows, width)
        return_send(j, slot)

    def home(j):
        combine(j, lax.rem(j, STG))
        rs_first(j)

    def finish_jv(j, h):
        jv = rs_final(j, h) + g[nch + j, mz, part(h)].astype(F32)
        jvf[j, part(h)] = jv
        ssacc[part(h)] += jv * jv
        g[j, mz, part(h)] = jv.astype(BF16)
        ag_first(j, h)

    def spread_jv(j):
        rs_drain(j)
        ag_done(j)
        dispatch(j, lax.rem(j, STG))
        dispatch_send(j, lax.rem(j, STG))

    contract_last = (((1,), (1,)), ((), ()))

    def back(j):
        dispatch_wait(j, lax.rem(j, STG))
        ag_drain(j)
        got = r[j].reshape(total, width)
        for n in range(ff // width):
            cols = slice(n * width, (n + 1) * width)
            acc[2, :, cols] += lax.dot_general(
                got, wd[j, cols, :], contract_last, preferred_element_type=F32
            )

    rl = YL
    al = rl + HB * half

    def tick_b(t, carry):
        for h in range(NS):
            at(al + HB * (half - 1), nch, t, lambda j, h=h: ag_far(j, h))
            for s in range(half - 1, 1, -1):
                at(al + HB * (s - 1), nch, t, lambda j, s=s, h=h: ag_mid(j, s, h))
            for s in range(half - 1, 1, -1):
                at(rl + HB * s, nch, t, lambda j, s=s, h=h: rs_mid(j, s, h))
            at(rl + HB, nch, t, lambda j, h=h: rs_second(j, h))
            at(al, nch, t, lambda j, h=h: finish_jv(j, h))
            if h == 0:
                at(al + HB * half, nch, t, spread_jv)
                at(rl, nch, t, home)
        at(0, nch, t, tangent_out)
        at(al + HB * half + YL, nch, t, back)
        return carry

    lax.fori_loop(0, nch + al + HB * half + YL, tick_b, 0)

    def exchange(stage, me_slot, count, dev_of):
        for k in range(1, count):
            d = lax.rem(me_slot + k, count)
            pltpu.make_async_remote_copy(
                src_ref=red.at[stage, me_slot], dst_ref=red.at[stage, me_slot],
                send_sem=red_sem.at[0, stage], recv_sem=red_sem.at[1, stage],
                device_id=dev_of(d), device_id_type=MESH,
            ).start()

    def gathered(stage, count):
        span = red.at[stage, pl.ds(0, count - 1)]
        local(span, span, red_sem.at[1, stage]).wait()
        local(span, span, red_sem.at[0, stage]).wait()
        value = red[stage, 0]
        for k in range(1, count):
            value = value + red[stage, k]
        return value

    squares = jnp.sum(jnp.sum(ssacc[...], axis=1, keepdims=True), axis=0, keepdims=True)
    red[0, mp] = jnp.broadcast_to(squares, (8, 128))
    if peers > 1:
        exchange(0, mp, peers, lambda d: {"expert": pdev(d)})

    @pl.loop(0, total // 16)
    def _(q):
        at_rows = pl.ds(pl.multiple_of(q * 16, 16), 16)
        gl = grecv[q // (rows // 16), pl.ds(pl.multiple_of(lax.rem(q, rows // 16) * 16, 16), 16), :]
        bk = acc[2, at_rows, :] * jnp.concatenate([gl] * (ff // tok), axis=1)
        gru[0, at_rows, :] = (bk * acc[1, at_rows, :]).astype(BF16)
        gru[1, at_rows, :] = (bk * acc[0, at_rows, :]).astype(BF16)

    def grad_out(j):
        slot = lax.rem(j, STG)
        pg = lax.dot_general(gru[0], wg[j], contract_last, preferred_element_type=F32)
        pg = pg + lax.dot_general(gru[1], wu[j], contract_last, preferred_element_type=F32)
        rstg[slot] = pg.astype(BF16).reshape(peers, rows, width)
        return_send(j, slot)

    def out_copy(j, slot):
        return local(ostg.at[slot], out_hbm.at[:, pl.ds(pl.multiple_of(j * width, width), width)], o_sem.at[slot])

    def finish_out(j, h):
        slot = lax.rem(j, 2)
        if h == 0:
            @pl.when(j >= 2)
            def _():
                out_copy(j - 2, slot).wait()

        mean = red[3, 0][0:1, 0:1] * (1.0 / (tok * nx * ny * nz * 2.0 * nch * width))
        scale = jnp.broadcast_to(lax.rsqrt(mean + 1e-06), (part_rows, width))
        ostg[slot, part(h)] = (rs_final(j, h) + jvf[j, part(h)]) * scale
        if h == NS - 1:
            out_copy(j, slot).start()

    dl = rl + HD * half

    def tick_d(t, carry):
        for h in range(NS):
            for s in range(half - 1, 1, -1):
                at(rl + HD * s, nch, t, lambda j, s=s, h=h: rs_mid(j, s, h))
            at(rl + HD, nch, t, lambda j, h=h: rs_second(j, h))
            if h == 0:
                at(rl, nch, t, home)
        at(0, nch, t, grad_out)

        @pl.when(t == 1)
        def _():
            red[1, mz] = gathered(0, peers)
            exchange(1, mz, nz, lambda d: {"expert": zdev(d)})

        @pl.when(t == rl + 1)
        def _():
            red[2, mx] = gathered(1, nz)
            if nx > 1:
                exchange(2, mx, nx, lambda d: {"dp": d})

        @pl.when(t == dl)
        def _():
            red[3, 0] = gathered(2, nx) if nx > 1 else red[2, 0]

        for h in range(NS):
            at(dl, nch, t, lambda j, h=h: finish_out(j, h))
        return carry

    lax.fori_loop(0, nch + dl, tick_d, 0)
    for j in range(nch):
        rs_drain(j)
    for j in range(max(0, nch - 2), nch):
        out_copy(j, j % 2).wait()


def shards(ny, nz, nx, tokens, tangent, routes, gates, w_gate, w_up, w_down):
    tok, depth = tokens.shape
    ff = w_gate.shape[2]
    width = 256
    nch = depth // width
    peers = 2 * ny
    rows = -(-(nz * CAP) // 16) * 16
    total = peers * rows
    slots = max(nz, peers, nx)
    dma = pltpu.SemaphoreType.DMA
    scratch = [
        pltpu.VMEM((nch, width, ff), BF16),
        pltpu.VMEM((nch, width, ff), BF16),
        pltpu.VMEM((nch, ff, width), BF16),
        pltpu.VMEM((2 * nch, nz, tok, width), BF16),
        pltpu.VMEM((2 * nch, peers, rows, width), BF16),
        pltpu.VMEM((total, nz * tok), BF16),
        pltpu.VMEM((nz * tok, total), BF16),
        pltpu.VMEM((4, total, ff), F32),
        pltpu.VMEM((total, ff), BF16),
        pltpu.VMEM((2, total, ff), BF16),
        pltpu.VMEM((nch, peers, rows, width), BF16),
        pltpu.VMEM((nch, nz, tok, width), BF16),
        pltpu.VMEM((nch, nz - 1, tok, width), BF16),
        pltpu.VMEM((STG, peers, rows, width), BF16),
        pltpu.VMEM((STG, peers, rows, width), BF16),
        pltpu.VMEM((nch, tok, width), F32),
        pltpu.VMEM((2, tok, width), F32),
        pltpu.VMEM((nz, 2 * peers, tok), F32),
        pltpu.VMEM((nz, 2 * peers, tok), F32),
        pltpu.VMEM((peers, rows, tok), F32),
        pltpu.VMEM((peers, rows, tok), F32),
        pltpu.VMEM((4, slots, 8, 128), F32),
        pltpu.VMEM((tok, width), F32),
        dma((2 * nch,)),
        dma((3,)),
        dma((2 * nch, nz - 1, NS)),
        dma((2 * nch,)),
        dma((2 * nch,)),
        dma((STG,)),
        dma((nch,)),
        dma((STG,)),
        dma((nch, nz - 1, NS)),
        dma((nch,)),
        dma((2,)),
        dma((2,)),
        dma((2,)),
        dma((2, 3)),
    ]
    anywhere = pl.BlockSpec(memory_space=pl.ANY)
    vmem = pl.BlockSpec(memory_space=pltpu.VMEM)
    return pl.pallas_call(
        functools.partial(body, ny, nz, nx, (tok, width, rows, nch, ff)),
        out_shape=jax.ShapeDtypeStruct((tok, depth), F32),
        in_specs=[anywhere, anywhere, vmem, vmem, anywhere, anywhere, anywhere],
        out_specs=anywhere,
        scratch_shapes=scratch,
        compiler_params=pltpu.CompilerParams(
            collective_id=0, has_side_effects=True, vmem_limit_bytes=67043328
        ),
        name="gauss_newton_moe",
    )(tokens, tangent, routes.T, gates.T, w_gate, w_up, w_down)


def build(mesh, ny, nz):
    placed = (
        P(("dp", "expert"), None),
        P(("dp", "expert"), None),
        P(("dp", "expert"), None),
        P(("dp", "expert"), None),
        P("expert", None, None),
        P("expert", None, None),
        P("expert", None, None),
    )
    return jax.shard_map(
        functools.partial(shards, ny, nz, mesh.shape["dp"]),
        mesh=mesh,
        in_specs=placed,
        out_specs=P(("dp", "expert"), None),
        check_vma=False,
    )


def solution(mesh):
    return build(mesh, 4, 8)
```
